32 devices in a mesh: tm: 4 (over x, core), vox: 8 (over z, y).
Axes of the slice: x: 2, y: 2, z: 4, core: 2. Of those that a mesh axis runs over, the one named last changes fastest.
Arguments:
- clip_features: bfloat16 [1024, 1024], P('tm'), may hold values from -6 to 6
- depth_kernel: float32 [3, 1024], replicated, may hold values from -3.5 to 3.5
- point_weight: bfloat16 [1024, 1024], replicated, may hold values from -0.1875 to 0.1875
- session_lengths: int32 [8], replicated, may hold values from 1 to 256, 1024 in all
- subject_feature_gains: float32 [16, 1024], replicated, may hold values from 0.25 to 1.75
- readout_weight: bfloat16 [1024, 5120], P(None, 'vox'), may hold values from -0.1875 to 0.1875
- hrf_kernel: float32 [16, 5120], P(None, 'vox'), may hold values from -1.5 to 1.5
- block_subject: int32 [40], P('vox'), may hold values from 0 to 15, as said below
- block_live: int32 [40], P('vox'), may hold values from 0 to 128, as said below
- bold_target: bfloat16 [1024, 5120], P('tm', 'vox'), may hold values from -6 to 6
Outputs:
- loss_total: float32 [], replicated
- grad_readout: float32 [1024, 5120], P('tm', 'vox')
- grad_point: float32 [1024, 1024], P(None, 'vox')
The draws below stay inside these ranges and needn't reach their ends.
Inputs may be any that keep to these rules, and one draw needn't show every extreme that they name: `session_lengths`: the lengths sum to 1024; one session has exactly 256 TRs. `block_subject`: ids never fall along the blocks; every subject owns one or two consecutive blocks, subject 0 two; the blocks after the last subject's live ones carry id 16 - 1 and no live voxels. `block_live`: the live voxels of a block are its first slots; a subject's blocks are full except its last, which holds at least one live voxel; blocks after the subjects' blocks are empty.
All inputs are finite; a program needn't handle non-finite values.
Results may differ from the reference program's by a relative error of at most 0.0044.
Values may be sent and summed in bfloat16 or wider, within the bound.
No kernel may reach another device: no remote copies, remote signals or barrier semaphores. Data moves between devices by JAX's collectives and lax.ppermute only.
A program may use at most 64 MiB of HBM per device.

```python
import math
import jax
import jax.numpy as jnp
import numpy as np
from jax import lax

FEAT = 1024
T_DEV = 256
BLOCK_VOX = 128
KERNEL_TAPS = 3
TAP_SPACING = 8
HRF = 16
TRS = 1024
VOXELS = 5120
BLOCKS = 40
SUBJ = 16
SESSIONS = 8


def block_layout(key):
    base_key = jax.random.fold_in(key, 7)
    extra_blocks = jax.random.randint(base_key, (SUBJ,), 0, 2).astype(jnp.int32)
    extra_blocks = extra_blocks.at[0].set(1)
    block_ends = jnp.cumsum(1 + extra_blocks).astype(jnp.int32)
    block_index = jnp.arange(BLOCKS, dtype=jnp.int32)
    subject_ids = jnp.sum((block_ends[None, :] <= block_index[:, None]).astype(jnp.int32), axis=1)
    subject_ids = jnp.minimum(subject_ids, SUBJ - 1)
    partial_fill = jax.random.randint(jax.random.fold_in(base_key, 11), (BLOCKS,), 1, BLOCK_VOX + 1).astype(jnp.int32)
    last_block = jnp.sum((block_ends[None, :] - 1 == block_index[:, None]).astype(jnp.int32), axis=1)
    live_counts = jnp.where(block_index < block_ends[SUBJ - 1], jnp.where(last_block > 0, partial_fill, BLOCK_VOX), 0)
    return (subject_ids.astype(jnp.int32), live_counts.astype(jnp.int32))


def draw_block_subject(key, part):
    return block_layout(key)[0]


def draw_block_live(key, part):
    return block_layout(key)[1]


def block_levels(own_key, shape, pieces, least, top_value):
    loudness, own = 1.0, jax.random.fold_in(own_key, 6)
    for axis_at, blocks in pieces:
        heights = jnp.exp(jax.random.uniform(jax.random.fold_in(own, axis_at), (blocks,), jnp.float32, least / len(pieces), top_value / len(pieces)))
        loudness = loudness * jnp.repeat(heights, shape[axis_at] // blocks).reshape([-1 if axis == axis_at else 1 for axis in range(len(shape))])
    return loudness


def length_profile(amount, total, limit, skew):
    portions = [(1 << 20) // math.isqrt(rank ** skew) + 1 for rank in range(2, amount + 1)]
    spare, holding = total - limit - (amount - 1), [1] * (amount - 1)
    while spare > 0:
        movable = [i for i in range(amount - 1) if holding[i] < limit]
        whole, budget = sum([portions[i] for i in movable]), spare
        for i in movable:
            addition = min(limit - holding[i], max(1, budget * portions[i] // whole), spare)
            holding[i] = holding[i] + addition
            spare = spare - addition
    return np.array([limit] + holding)


def ragged_sizes(own_key, number_of, total, most, skew):
    if number_of == 2:
        one = jax.random.randint(own_key, (), max(1, total - most), min(most, total - 1) + 1)
        return jnp.stack([one, total - one])
    lengths = jnp.asarray(length_profile(number_of, total, most, skew), jnp.int32)
    twos = (number_of - 1) // 2
    giver, sink = lengths[1:1 + 2 * twos:2], lengths[2:2 + 2 * twos:2]
    margin = jnp.minimum(giver - 1, most - sink)
    shifted = jax.random.randint(jax.random.fold_in(own_key, 1), (twos,), 0, 1 << 20) % (margin + 1)
    lengths = lengths.at[1:1 + 2 * twos:2].set(giver - shifted).at[2:2 + 2 * twos:2].set(sink + shifted)
    return lengths[jax.random.permutation(jax.random.fold_in(own_key, 2), number_of)]


def centred(stream_key, shape, scale, reach, pieces=(), kind=jnp.bfloat16):
    gain = block_levels(stream_key, shape, pieces, -0.22, 0.18) if pieces else 1.0
    entries = jax.random.normal(stream_key, shape, jnp.float32) * scale * gain
    return jnp.minimum(jnp.maximum(entries, -reach), reach).astype(kind)


def setup_inputs(seed: int = 0) -> dict:
    key_of = jax.random.split(jax.random.key(seed), 11)
    clip_features = centred(key_of[0], (TRS, FEAT), 1.0, 6.0, ((0, 4),))
    depth_kernel = centred(key_of[1], (KERNEL_TAPS, FEAT), KERNEL_TAPS ** -0.5, 3.5, (), jnp.float32)
    point_weight = centred(key_of[2], (FEAT, FEAT), FEAT ** -0.5, 0.1875)
    session_lengths = ragged_sizes(key_of[3], SESSIONS, TRS, T_DEV, 2).astype(jnp.int32)
    subject_feature_gains = jnp.clip(1.0 + 0.15 * jax.random.normal(key_of[4], (SUBJ, FEAT), jnp.float32), 0.25, 1.75)
    readout_weight = centred(key_of[5], (FEAT, VOXELS), FEAT ** -0.5, 0.1875, ((1, 8),))
    hrf_kernel = centred(key_of[6], (HRF, VOXELS), 0.25, 1.5, ((1, 8),), jnp.float32)
    block_subject = draw_block_subject(jax.random.fold_in(key_of[10], 71), 0)
    block_live = draw_block_live(jax.random.fold_in(key_of[10], 71), 0)
    bold_target = centred(key_of[9], (TRS, VOXELS), 1.0, 6.0, ((0, 4), (1, 8)))
    return {"clip_features": clip_features, "depth_kernel": depth_kernel, "point_weight": point_weight, "session_lengths": session_lengths, "subject_feature_gains": subject_feature_gains, "readout_weight": readout_weight, "hrf_kernel": hrf_kernel, "block_subject": block_subject, "block_live": block_live, "bold_target": bold_target}


def reference(clip_features, depth_kernel, point_weight, session_lengths, subject_feature_gains, readout_weight, hrf_kernel, block_subject, block_live, bold_target):
    position = jnp.arange(TRS, dtype=jnp.int32)
    session_ends = jnp.cumsum(session_lengths).astype(jnp.int32)
    session = lax.optimization_barrier(jnp.sum((session_ends[None, :] <= position[:, None]).astype(jnp.int32), axis=1))
    source_x = clip_features.astype(jnp.float32)
    depth_sum = jnp.zeros((TRS, FEAT), jnp.float32)
    for kernel_tap_index in range(KERNEL_TAPS):
        delayed_rows = kernel_tap_index * TAP_SPACING
        moved = jnp.concatenate([jnp.zeros((delayed_rows, FEAT), jnp.float32), source_x[:TRS - delayed_rows]], axis=0)
        moved_session = jnp.concatenate([jnp.full((delayed_rows,), -1, jnp.int32), session[:TRS - delayed_rows]])
        valid_tap = moved_session == session
        depth_sum = depth_sum + depth_kernel[kernel_tap_index][None, :] * jnp.where(valid_tap[:, None], moved, 0.0)
    depth_half = depth_sum.astype(jnp.bfloat16)
    pre_act = jnp.dot(depth_half, point_weight, preferred_element_type=jnp.float32)
    core_out = (source_x + jax.nn.gelu(pre_act)).astype(jnp.bfloat16)
    gain_rows = subject_feature_gains[block_subject]
    scale_cols = jnp.transpose(gain_rows)[:, :, None]
    effective = (readout_weight.astype(jnp.float32).reshape(FEAT, BLOCKS, BLOCK_VOX) * scale_cols).reshape(FEAT, VOXELS).astype(jnp.bfloat16)
    response = jnp.dot(core_out, effective, preferred_element_type=jnp.float32).astype(jnp.bfloat16)
    response_wide = response.astype(jnp.float32)
    predicted = jnp.zeros((TRS, VOXELS), jnp.float32)
    for kernel_tap_index in range(HRF):
        moved = jnp.concatenate([jnp.zeros((kernel_tap_index, VOXELS), jnp.float32), response_wide[:TRS - kernel_tap_index]], axis=0)
        moved_session = jnp.concatenate([jnp.full((kernel_tap_index,), -1, jnp.int32), session[:TRS - kernel_tap_index]])
        valid_tap = moved_session == session
        predicted = predicted + hrf_kernel[kernel_tap_index][None, :] * jnp.where(valid_tap[:, None], moved, 0.0)
    subject_voxels = jnp.zeros((SUBJ,), jnp.float32).at[block_subject].add(block_live.astype(jnp.float32))
    live_mask = (jnp.arange(BLOCK_VOX, dtype=jnp.int32)[None, :] < block_live[:, None]).astype(jnp.float32).reshape(VOXELS)
    voxel_count = jnp.repeat(subject_voxels[block_subject], BLOCK_VOX)
    voxel_weight = live_mask / voxel_count
    misfit = predicted - bold_target.astype(jnp.float32)
    loss_total = jnp.sum(voxel_weight[None, :] * misfit * misfit) / (SUBJ * TRS)
    pred_grad = 2.0 * voxel_weight[None, :] * misfit
    response_grad = jnp.zeros((TRS, VOXELS), jnp.float32)
    for kernel_tap_index in range(HRF):
        moved = jnp.concatenate([pred_grad[kernel_tap_index:], jnp.zeros((kernel_tap_index, VOXELS), jnp.float32)], axis=0)
        moved_session = jnp.concatenate([session[kernel_tap_index:], jnp.full((kernel_tap_index,), -1, jnp.int32)])
        valid_tap = moved_session == session
        response_grad = response_grad + hrf_kernel[kernel_tap_index][None, :] * jnp.where(valid_tap[:, None], moved, 0.0)
    response_half = response_grad.astype(jnp.bfloat16)
    readout_raw = lax.dot_general(core_out, response_half, (((0,), (0,)), ((), ())), preferred_element_type=jnp.float32)
    grad_readout = (readout_raw.reshape(FEAT, BLOCKS, BLOCK_VOX) * scale_cols).reshape(FEAT, VOXELS)
    core_grad = lax.dot_general(response_half, effective, (((1,), (1,)), ((), ())), preferred_element_type=jnp.float32)
    pre_grad = jax.vjp(jax.nn.gelu, pre_act)[1](core_grad)[0].astype(jnp.bfloat16)
    grad_point = lax.dot_general(depth_half, pre_grad, (((0,), (0,)), ((), ())), preferred_element_type=jnp.float32)
    return (loss_total, grad_readout, grad_point)
```

```python
import functools
import jax
import jax.numpy as jnp
from jax import lax
from jax.experimental import pallas as pl
from jax.experimental.pallas import tpu as pltpu
from jax.sharding import PartitionSpec as P

BLOCK_VOX = 128
KERNEL_TAPS = 3
TAP_SPACING = 8
HRF = 16
MARGIN = (KERNEL_TAPS - 1) * TAP_SPACING
F32 = jnp.float32
BF16 = jnp.bfloat16
NT = (((1,), (1,)), ((), ()))
VMEM = pl.BlockSpec(memory_space=pltpu.VMEM)
SMEM = pl.BlockSpec(memory_space=pltpu.SMEM)


def call(body, outs, ins, flops, moved, scratch=()):
    return pl.pallas_call(
        body,
        out_shape=outs,
        in_specs=[spec for spec, _ in ins],
        out_specs=jax.tree.map(lambda _: VMEM, outs),
        scratch_shapes=scratch,
        compiler_params=pltpu.CompilerParams(vmem_limit_bytes=40 << 20),
        cost_estimate=pl.CostEstimate(flops=flops, bytes_accessed=moved, transcendentals=0),
    )(*[value for _, value in ins])


def session_starts(lengths_ref, time):
    start = jnp.zeros_like(time)
    end = jnp.int32(0)
    for at in range(lengths_ref.shape[0]):
        end = end + lengths_ref[at]
        start = jnp.where(time >= end, end, start)
    return start


def session_stops(lengths_ref, time):
    stop = jnp.zeros_like(time)
    ends = []
    end = jnp.int32(0)
    for at in range(lengths_ref.shape[0]):
        end = end + lengths_ref[at]
        ends.append(end)
    for end in reversed(ends):
        stop = jnp.where(time < end, end, stop)
    return stop


def gain_kernel(blocks, subject_ref, gains_ref, weight_ref, effective_ref):
    rows = [gains_ref[pl.ds(subject_ref[b], 1), :] for b in range(blocks)]
    rows += [rows[-1]] * (-blocks % 8)
    cols = jnp.transpose(jnp.concatenate(rows, axis=0))
    for b in range(blocks):
        lanes = slice(b * BLOCK_VOX, (b + 1) * BLOCK_VOX)
        effective_ref[:, lanes] = (
            weight_ref[:, lanes].astype(F32) * cols[:, b : b + 1]
        ).astype(BF16)


def core_kernel(
    rows, lengths_ref, clip_ref, near_ref, far_ref, taps_ref, point_ref, depth_ref, core_ref, ext, deep
):
    feats = clip_ref.shape[1]
    odd = lax.axis_index("tm") % 2
    ext[2 * MARGIN : 2 * MARGIN + rows, :] = clip_ref[...]

    @pl.when(odd == 0)
    def _():
        ext[: 2 * MARGIN, :] = far_ref[: 2 * MARGIN, :]
        ext[2 * MARGIN + rows :, :] = near_ref[2 * MARGIN : 3 * MARGIN, :]

    @pl.when(odd == 1)
    def _():
        ext[: 2 * MARGIN, :] = near_ref[: 2 * MARGIN, :]
        ext[2 * MARGIN + rows :, :] = far_ref[2 * MARGIN : 3 * MARGIN, :]

    first = lax.axis_index("tm") * rows - MARGIN
    taps = [taps_ref[k : k + 1, :] for k in range(KERNEL_TAPS)]
    for at in range(0, rows + 2 * MARGIN, 16):
        time = first + at + lax.broadcasted_iota(jnp.int32, (16, 128), 0)
        since = time - session_starts(lengths_ref, time)
        values = ext[at : at + 32, :].astype(F32)
        total = taps[0] * values[16:32]
        for k in range(1, KERNEL_TAPS):
            valid = (since >= k * TAP_SPACING).astype(F32)
            shift = MARGIN - k * TAP_SPACING
            moved = values[shift : shift + 16] * jnp.tile(valid, (1, feats // 128))
            total = total + taps[k] * moved
        deep[at : at + 16, :] = total.astype(BF16)
    depth_ref[...] = deep[MARGIN : MARGIN + rows, :]
    for col in range(0, feats, 256):
        lanes = slice(col, col + 256)
        act = jnp.dot(deep[...], point_ref[:, lanes], preferred_element_type=F32)
        core_ref[:, lanes] = (
            ext[MARGIN : MARGIN + rows + 2 * MARGIN, lanes].astype(F32) + jax.nn.gelu(act)
        ).astype(BF16)


def block_at(position, bits):
    return sum(
        ((position >> (len(bits) - 1 - s)) & 1) << bits[s] for s in range(len(bits))
    )


def picked(position, orders):
    even, odd = (block_at(position, bits) for bits in orders)
    mask = jnp.where(lax.axis_index("tm") % 2 == 0, even, odd)
    return lax.axis_index("vox") ^ mask


def voxel_kernel(
    rows,
    blocks,
    orders,
    width,
    lengths_ref,
    own_ref,
    mine_ref,
    twin_ref,
    core_ref,
    effective_ref,
    hrf_ref,
    bold_ref,
    near_ref,
    far_ref,
    half_ref,
    send_ref,
    loss_ref,
    response,
    grads,
    bold,
    since,
    left,
    scale,
):
    ext_rows = rows + 2 * MARGIN
    lead_rows = rows + MARGIN
    slots = blocks * BLOCK_VOX
    odd = lax.axis_index("tm") % 2
    bold[:rows, :] = bold_ref[...]

    @pl.when(odd == 0)
    def _():
        bold[rows:, :] = near_ref[3 * MARGIN :, :slots]

    @pl.when(odd == 1)
    def _():
        bold[rows:, :] = far_ref[3 * MARGIN :, :slots]

    first = lax.axis_index("tm") * rows
    time = first + lax.broadcasted_iota(jnp.int32, (lead_rows, 128), 0)
    since[...] = time - session_starts(lengths_ref, time)
    left[...] = session_stops(lengths_ref, time) - 1 - time

    even_vox = lax.axis_index("vox") % 2 == 0
    zero_odd = odd == 0

    def neighbour(at):
        low = jnp.where(zero_odd, mine_ref[at], twin_ref[at])
        high = jnp.where(zero_odd, twin_ref[at], mine_ref[at])
        return low, high

    last_pair = [neighbour(blocks - 1), neighbour(2 * blocks - 1)]
    next_pair = [neighbour(0), neighbour(blocks)]
    before = [jnp.where(even_vox, high, low) for low, high in last_pair]
    after = [jnp.where(even_vox, low, high) for low, high in next_pair]
    subjects = [before[0]] + [own_ref[b] for b in range(blocks)] + [after[0]]
    lives = [before[1]] + [own_ref[blocks + b] for b in range(blocks)] + [after[1]]
    lane = lax.broadcasted_iota(jnp.int32, (16, BLOCK_VOX), 1)
    for b in range(blocks):
        count = lives[b + 1]
        count = count + jnp.where(subjects[b] == subjects[b + 1], lives[b], 0)
        count = count + jnp.where(subjects[b + 2] == subjects[b + 1], lives[b + 2], 0)
        counts = jnp.full((16, BLOCK_VOX), jnp.maximum(count, 1), jnp.int32).astype(F32)
        scale[b] = jnp.where(lane < lives[b + 1], 1.0 / counts, 0.0)

    for b in range(0, blocks, 2):
        many = min(2, blocks - b)
        lanes = slice(b * BLOCK_VOX, (b + many) * BLOCK_VOX)
        part = jnp.dot(core_ref[...], effective_ref[:, lanes], preferred_element_type=F32)
        part = part.astype(BF16).astype(F32)
        for c in range(many):
            response[b + c] = part[:, c * BLOCK_VOX : (c + 1) * BLOCK_VOX]

    def one_block(b, lost):
        lanes = pl.ds(pl.multiple_of(b * BLOCK_VOX, BLOCK_VOX), BLOCK_VOX)
        taps = [jnp.broadcast_to(hrf_ref[k : k + 1, lanes], (16, BLOCK_VOX)) for k in range(HRF)]
        weight = scale[b]
        double = 2.0 * weight
        for at in range(0, lead_rows, 16):
            depth = since[at : at + 16, :]
            total = taps[0] * response[b, MARGIN + at : MARGIN + at + 16, :]
            for k in range(1, HRF):
                moved = response[b, MARGIN + at - k : MARGIN + at - k + 16, :]
                total = total + taps[k] * jnp.where(depth >= k, moved, 0.0)
            misfit = total - bold[at : at + 16, lanes].astype(F32)
            grads[b, at : at + 16, :] = double * misfit
            if at < rows:
                cost = weight * misfit * misfit
                lost = lost + cost[:8] + cost[8:]
        for at in range(0, rows, 16):
            depth = left[at : at + 16, :]
            total = taps[0] * grads[b, at : at + 16, :]
            for k in range(1, HRF):
                moved = grads[b, at + k : at + k + 16, :]
                total = total + taps[k] * jnp.where(depth >= k, moved, 0.0)
            half_ref[at : at + 16, lanes] = total.astype(BF16)
        return lost

    lost = lax.fori_loop(0, blocks, one_block, jnp.zeros((8, BLOCK_VOX), F32))
    loss_ref[...] = lost
    high = lost.astype(BF16).astype(F32)
    pair = jnp.concatenate([high, lost - high], axis=0)
    pad = jnp.zeros((16, rows - BLOCK_VOX), F32)
    pieces = 1 << len(orders[0])
    halves = pieces // 2
    send_ref[halves * width :, :] = jnp.concatenate([pair, pad], axis=1).astype(BF16)
    for p in range(halves):
        at = pl.multiple_of(picked(halves + p, orders) * width, width)
        send_ref[p * width : (p + 1) * width, :] = lax.dot_general(
            effective_ref[pl.ds(at, width), :], half_ref[...], NT, preferred_element_type=F32
        ).astype(BF16)


def rest_kernel(
    rows, orders, width, tm_bits, share, core_ref, effective_ref, half_ref, keep_ref, out_ref, own_ref, flipped
):
    halves = 1 << (len(orders[0]) - 1)
    flipped[...] = jnp.transpose(core_ref[MARGIN : MARGIN + rows, :])
    pieces = 1 << len(tm_bits)
    for q in reversed(range(pieces)):
        at = pl.multiple_of((lax.axis_index("tm") ^ block_at(q, tm_bits)) * share, share)
        part = jnp.dot(flipped[pl.ds(at, share), :], half_ref[...], preferred_element_type=F32)
        if q >= pieces // 2:
            slot = q - pieces // 2
            out_ref[slot * share : (slot + 1) * share, :] = part.astype(BF16)
        else:
            own_ref[q * share : (q + 1) * share, :] = part
    for p in range(halves):
        at = pl.multiple_of(picked(p, orders) * width, width)
        keep_ref[p * width : (p + 1) * width, :] = lax.dot_general(
            effective_ref[pl.ds(at, width), :], half_ref[...], NT, preferred_element_type=F32
        )


def last_kernel(parts, width, grads_ref, *refs):
    depth_refs, (point_ref,) = refs[:parts], refs[parts:]
    feats = point_ref.shape[0]
    for col in range(0, feats, 256):
        lanes = slice(col, col + 256)
        total = None
        for r in range(parts):
            part = jnp.dot(
                grads_ref[r, :width, :], depth_refs[r][:, lanes], preferred_element_type=F32
            )
            total = part if total is None else total + part
        point_ref[lanes, :] = jnp.transpose(total)


def shards(
    tm_count,
    vox_count,
    clip_features,
    depth_kernel,
    point_weight,
    session_lengths,
    subject_feature_gains,
    readout_weight,
    hrf_kernel,
    block_subject,
    block_live,
    bold_target,
):
    rows, feats = clip_features.shape
    slots = readout_weight.shape[1]
    blocks = slots // BLOCK_VOX
    subjects = subject_feature_gains.shape[0]
    width = feats // vox_count
    share = feats // tm_count
    vox_bits = list(range(vox_count.bit_length() - 1))
    orders = (vox_bits, [vox_bits[1], vox_bits[0]] + vox_bits[2:])
    tm_bits = list(range(tm_count.bit_length() - 1))

    def swap_tm(value, bit):
        return lax.ppermute(value, "tm", [(i, i ^ (1 << bit)) for i in range(tm_count)])

    def across(value, partner):
        pairs = []
        for t in range(tm_count):
            for v in range(vox_count):
                to = partner(t, v)
                if to is not None:
                    pairs.append((t * vox_count + v, to[0] * vox_count + to[1]))
        return lax.ppermute(value, ("tm", "vox"), pairs)

    def next_tm(t, v):
        other = t + 1 if t % 2 else t - 1
        return (other, v) if 0 <= other < tm_count else None

    def next_vox(t, v):
        if t % 2 == 0:
            return (t, v ^ 1)
        other = v + 1 if v % 2 else v - 1
        return (t, other) if 0 <= other < vox_count else None

    payload = jnp.concatenate(
        [
            clip_features[rows - 2 * MARGIN :],
            clip_features[:MARGIN],
            jnp.pad(bold_target[:MARGIN], ((0, 0), (0, feats - slots))),
        ],
        axis=0,
    )
    far = across(payload, next_tm)
    own_blocks = jnp.concatenate([block_subject, block_live])
    mine = across(own_blocks, next_vox)
    near = swap_tm(payload, 0)
    twin = swap_tm(mine, 0)

    effective = call(
        functools.partial(gain_kernel, blocks),
        jax.ShapeDtypeStruct((feats, slots), BF16),
        [(SMEM, block_subject), (VMEM, subject_feature_gains), (VMEM, readout_weight)],
        feats * slots,
        4 * feats * slots,
    )
    depth_half, core_out = call(
        functools.partial(core_kernel, rows),
        (
            jax.ShapeDtypeStruct((rows, feats), BF16),
            jax.ShapeDtypeStruct((rows + 2 * MARGIN, feats), BF16),
        ),
        [
            (SMEM, session_lengths),
            (VMEM, clip_features),
            (VMEM, near),
            (VMEM, far),
            (VMEM, depth_kernel),
            (VMEM, point_weight),
        ],
        2 * rows * feats * feats,
        2 * feats * feats,
        [
            pltpu.VMEM((rows + 3 * MARGIN, feats), BF16),
            pltpu.VMEM((rows + 2 * MARGIN, feats), BF16),
        ],
    )
    half, send, lost = call(
        functools.partial(voxel_kernel, rows, blocks, orders, width),
        (
            jax.ShapeDtypeStruct((rows, slots), BF16),
            jax.ShapeDtypeStruct((feats // 2 + 16, rows), BF16),
            jax.ShapeDtypeStruct((8, BLOCK_VOX), F32),
        ),
        [
            (SMEM, session_lengths),
            (SMEM, own_blocks),
            (SMEM, mine),
            (SMEM, twin),
            (VMEM, core_out),
            (VMEM, effective),
            (VMEM, hrf_kernel),
            (VMEM, bold_target),
            (VMEM, near),
            (VMEM, far),
        ],
        4 * rows * feats * slots,
        8 * rows * slots,
        [
            pltpu.VMEM((blocks, rows + 2 * MARGIN, BLOCK_VOX), F32),
            pltpu.VMEM((blocks, rows + MARGIN, BLOCK_VOX), F32),
            pltpu.VMEM((rows + MARGIN, slots), BF16),
            pltpu.VMEM((rows + MARGIN, BLOCK_VOX), jnp.int32),
            pltpu.VMEM((rows + MARGIN, BLOCK_VOX), jnp.int32),
            pltpu.VMEM((blocks, 16, BLOCK_VOX), F32),
        ],
    )
    keep, raw_send, raw_keep = call(
        functools.partial(rest_kernel, rows, orders, width, tm_bits, share),
        (
            jax.ShapeDtypeStruct((feats // 2, rows), F32),
            jax.ShapeDtypeStruct((feats // 2, slots), BF16),
            jax.ShapeDtypeStruct((feats // 2, slots), F32),
        ),
        [(VMEM, core_out), (VMEM, effective), (VMEM, half)],
        4 * rows * feats * slots,
        8 * feats * slots,
        [pltpu.VMEM((feats, rows), BF16)],
    )

    def loss_rows(value):
        high = lax.reduce_precision(value, 8, 7)
        pair = jnp.concatenate([high, value - high], axis=0)
        return jnp.pad(pair, ((0, 0), (0, rows - BLOCK_VOX))).astype(BF16)

    def loss_of(arrived):
        pair = arrived[:, :BLOCK_VOX].astype(F32)
        return pair[:8] + pair[8:]

    for stage in range(len(vox_bits)):
        arrived = across(send, lambda t, v: (t, v ^ (1 << orders[t % 2][stage])))
        size = keep.shape[0]
        keep = keep + arrived[:size].astype(F32)
        lost = lost + loss_of(arrived[size:])
        if stage + 1 < len(vox_bits):
            send = jnp.concatenate([keep[size // 2 :].astype(BF16), loss_rows(lost)], axis=0)
            keep = keep[: size // 2]

    col = lax.axis_index("vox") * width
    point_cols = lax.dynamic_slice_in_dim(point_weight, col, width, 1)
    pre_act = lax.dot_general(
        point_cols, depth_half, (((0,), (1,)), ((), ())), preferred_element_type=F32
    )
    pre_grad = jax.vjp(jax.nn.gelu, pre_act)[1](keep)[0].astype(BF16)
    gathered = jnp.concatenate([pre_grad, loss_rows(lost)], axis=0)[None]
    depths = [depth_half]
    for bit in reversed(tm_bits):
        depths = depths + [swap_tm(value, bit) for value in depths]
        gathered = jnp.concatenate([gathered, swap_tm(gathered, bit)], axis=0)
    loss_sum = jnp.sum(gathered[:, width:, :BLOCK_VOX].astype(F32))
    loss_total = loss_sum / (subjects * rows * tm_count)
    grad_point = call(
        functools.partial(last_kernel, tm_count, width),
        jax.ShapeDtypeStruct((feats, width), F32),
        [(VMEM, gathered)] + [(VMEM, value) for value in depths],
        2 * rows * tm_count * feats * width,
        2 * rows * tm_count * feats,
    )

    for bit in tm_bits:
        arrived = swap_tm(raw_send, bit)
        raw_keep = raw_keep + arrived.astype(F32)
        if bit + 1 < len(tm_bits):
            size = raw_keep.shape[0] // 2
            raw_send = raw_keep[size:].astype(BF16)
            raw_keep = raw_keep[:size]
    own_gains = lax.dynamic_slice_in_dim(
        subject_feature_gains, lax.axis_index("tm") * share, share, 1
    )
    gain_cols = jnp.transpose(own_gains[block_subject])
    grad_readout = raw_keep * jnp.repeat(gain_cols, BLOCK_VOX, axis=1)
    return (loss_total, grad_readout, grad_point)


def solution(mesh):
    placed = (
        P("tm", None),
        P(),
        P(),
        P(),
        P(),
        P(None, "vox"),
        P(None, "vox"),
        P("vox"),
        P("vox"),
        P("tm", "vox"),
    )
    return jax.shard_map(
        functools.partial(shards, mesh.shape["tm"], mesh.shape["vox"]),
        mesh=mesh,
        in_specs=placed,
        out_specs=(P(), P("tm", "vox"), P(None, "vox")),
        check_vma=False,
    )
```

```python
import functools
import jax
import jax.numpy as jnp
from jax import lax
from jax.experimental import pallas as pl
from jax.experimental.pallas import tpu as pltpu
from jax.sharding import PartitionSpec as P

BLOCK_VOX = 128
KERNEL_TAPS = 3
TAP_SPACING = 8
HRF = 16
MARGIN = (KERNEL_TAPS - 1) * TAP_SPACING
F32 = jnp.float32
BF16 = jnp.bfloat16
NT = (((1,), (1,)), ((), ()))
VMEM = pl.BlockSpec(memory_space=pltpu.VMEM)
SMEM = pl.BlockSpec(memory_space=pltpu.SMEM)
HBM = pl.BlockSpec(memory_space=pltpu.HBM)


def call(body, outs, ins, micros, scratch=()):
    return pl.pallas_call(
        body,
        out_shape=outs,
        in_specs=[spec for spec, _ in ins],
        out_specs=jax.tree.map(lambda _: VMEM, outs),
        scratch_shapes=scratch,
        compiler_params=pltpu.CompilerParams(vmem_limit_bytes=16 << 20),
        cost_estimate=pl.CostEstimate(
            flops=int(micros * 1.15e9), bytes_accessed=int(micros * 1e6), transcendentals=0
        ),
    )(*[value for _, value in ins])


def session_starts(lengths_ref, time):
    start = jnp.zeros_like(time)
    end = jnp.int32(0)
    for at in range(lengths_ref.shape[0]):
        end = end + lengths_ref[at]
        start = jnp.where(time >= end, end, start)
    return start


def session_stops(lengths_ref, time):
    stop = jnp.zeros_like(time)
    ends = []
    end = jnp.int32(0)
    for at in range(lengths_ref.shape[0]):
        end = end + lengths_ref[at]
        ends.append(end)
    for end in reversed(ends):
        stop = jnp.where(time < end, end, stop)
    return stop


def pack_kernel(blocks, subject_ref, live_ref, tail_ref, head_ref, bold_ref, payload_ref, ends_ref):
    slots = bold_ref.shape[1]
    payload_ref[: 2 * MARGIN, :] = tail_ref[...]
    payload_ref[2 * MARGIN : 3 * MARGIN, :] = head_ref[...]
    payload_ref[3 * MARGIN :, :slots] = bold_ref[...]
    payload_ref[3 * MARGIN :, slots:] = jnp.zeros_like(payload_ref[3 * MARGIN :, slots:])
    row = lax.broadcasted_iota(jnp.int32, ends_ref.shape, 0)
    last = blocks - 1
    ends = jnp.where(row == 0, subject_ref[0], live_ref[0])
    ends = jnp.where(row == 2, subject_ref[last], ends)
    ends_ref[...] = jnp.where(row == 3, live_ref[last], ends)


def gain_kernel(blocks, subject_ref, gains_ref, weight_ref, effective_ref):
    rows = [gains_ref[pl.ds(subject_ref[b], 1), :] for b in range(blocks)]
    rows += [rows[-1]] * (-blocks % 8)
    cols = jnp.transpose(jnp.concatenate(rows, axis=0))
    for b in range(blocks):
        lanes = slice(b * BLOCK_VOX, (b + 1) * BLOCK_VOX)
        effective_ref[:, lanes] = (
            weight_ref[:, lanes].astype(F32) * cols[:, b : b + 1]
        ).astype(BF16)


def core_kernel(
    rows,
    lengths_ref,
    clip_ref,
    near_ref,
    far_ref,
    taps_ref,
    point_ref,
    depth_ref,
    core_ref,
    ext,
    deep,
):
    feats = clip_ref.shape[1]
    odd = lax.axis_index("tm") % 2
    ext[2 * MARGIN : 2 * MARGIN + rows, :] = clip_ref[...]

    @pl.when(odd == 0)
    def _():
        ext[: 2 * MARGIN, :] = far_ref[: 2 * MARGIN, :]
        ext[2 * MARGIN + rows :, :] = near_ref[2 * MARGIN : 3 * MARGIN, :]

    @pl.when(odd == 1)
    def _():
        ext[: 2 * MARGIN, :] = near_ref[: 2 * MARGIN, :]
        ext[2 * MARGIN + rows :, :] = far_ref[2 * MARGIN : 3 * MARGIN, :]

    first = lax.axis_index("tm") * rows - MARGIN
    taps = [taps_ref[k : k + 1, :] for k in range(KERNEL_TAPS)]
    for at in range(0, rows + 2 * MARGIN, 16):
        time = first + at + lax.broadcasted_iota(jnp.int32, (16, 128), 0)
        since = time - session_starts(lengths_ref, time)
        values = ext[at : at + 32, :].astype(F32)
        total = taps[0] * values[16:32]
        for k in range(1, KERNEL_TAPS):
            valid = (since >= k * TAP_SPACING).astype(F32)
            shift = MARGIN - k * TAP_SPACING
            moved = values[shift : shift + 16] * jnp.tile(valid, (1, feats // 128))
            total = total + taps[k] * moved
        deep[at : at + 16, :] = total.astype(BF16)
    depth_ref[...] = deep[MARGIN : MARGIN + rows, :]
    for col in range(0, feats, 256):
        lanes = slice(col, col + 256)
        act = jnp.dot(deep[...], point_ref[:, lanes], preferred_element_type=F32)
        core_ref[:, lanes] = (
            ext[MARGIN : MARGIN + rows + 2 * MARGIN, lanes].astype(F32) + jax.nn.gelu(act)
        ).astype(BF16)


def block_at(position, bits):
    return sum(
        ((position >> (len(bits) - 1 - s)) & 1) << bits[s] for s in range(len(bits))
    )


def picked(position, orders):
    even, odd = (block_at(position, bits) for bits in orders)
    mask = jnp.where(lax.axis_index("tm") % 2 == 0, even, odd)
    return lax.axis_index("vox") ^ mask


def voxel_kernel(
    rows,
    blocks,
    orders,
    width,
    lengths_ref,
    subject_ref,
    live_ref,
    mine_ref,
    twin_ref,
    core_ref,
    effective_ref,
    hrf_ref,
    bold_ref,
    near_ref,
    far_ref,
    half_ref,
    send_ref,
    loss_ref,
    response,
    grads,
    bold,
    since,
    left,
    scale,
):
    ext_rows = rows + 2 * MARGIN
    lead_rows = rows + MARGIN
    slots = blocks * BLOCK_VOX
    odd = lax.axis_index("tm") % 2
    bold[:rows, :] = bold_ref[...]

    @pl.when(odd == 0)
    def _():
        bold[rows:, :] = near_ref[3 * MARGIN :, :slots]

    @pl.when(odd == 1)
    def _():
        bold[rows:, :] = far_ref[3 * MARGIN :, :slots]

    first = lax.axis_index("tm") * rows
    time = first + lax.broadcasted_iota(jnp.int32, (lead_rows, 128), 0)
    since[...] = time - session_starts(lengths_ref, time)
    left[...] = session_stops(lengths_ref, time) - 1 - time

    first_core = odd == 0
    low = jnp.where(first_core, mine_ref[...], twin_ref[...])
    high = jnp.where(first_core, twin_ref[...], mine_ref[...])
    even_vox = lax.axis_index("vox") % 2 == 0
    before = jnp.where(even_vox, high, low)
    after = jnp.where(even_vox, low, high)
    subjects = [before[2:3]] + [subject_ref[b] for b in range(blocks)] + [after[0:1]]
    lives = [before[3:4]] + [live_ref[b] for b in range(blocks)] + [after[1:2]]
    lane = lax.broadcasted_iota(jnp.int32, (16, BLOCK_VOX), 1)
    for b in range(blocks):
        count = jnp.full((1, BLOCK_VOX), lives[b + 1], jnp.int32)
        count = count + jnp.where(subjects[b] == subjects[b + 1], lives[b], 0)
        count = count + jnp.where(subjects[b + 2] == subjects[b + 1], lives[b + 2], 0)
        inverse = 1.0 / jnp.maximum(count, 1).astype(F32)
        scale[b] = jnp.where(lane < lives[b + 1], inverse, 0.0)

    for b in range(0, blocks, 2):
        many = min(2, blocks - b)
        lanes = slice(b * BLOCK_VOX, (b + many) * BLOCK_VOX)
        part = jnp.dot(core_ref[...], effective_ref[:, lanes], preferred_element_type=F32)
        part = part.astype(BF16).astype(F32)
        for c in range(many):
            response[b + c] = part[:, c * BLOCK_VOX : (c + 1) * BLOCK_VOX]

    def one_block(b, lost):
        lanes = pl.ds(pl.multiple_of(b * BLOCK_VOX, BLOCK_VOX), BLOCK_VOX)
        taps = [jnp.broadcast_to(hrf_ref[k : k + 1, lanes], (16, BLOCK_VOX)) for k in range(HRF)]
        weight = scale[b]
        double = 2.0 * weight
        for at in range(0, lead_rows, 16):
            depth = since[at : at + 16, :]
            total = taps[0] * response[b, MARGIN + at : MARGIN + at + 16, :]
            for k in range(1, HRF):
                moved = response[b, MARGIN + at - k : MARGIN + at - k + 16, :]
                total = total + taps[k] * jnp.where(depth >= k, moved, 0.0)
            misfit = total - bold[at : at + 16, lanes].astype(F32)
            grads[b, at : at + 16, :] = double * misfit
            if at < rows:
                cost = weight * misfit * misfit
                lost = lost + cost[:8] + cost[8:]
        for at in range(0, rows, 16):
            depth = left[at : at + 16, :]
            total = taps[0] * grads[b, at : at + 16, :]
            for k in range(1, HRF):
                moved = grads[b, at + k : at + k + 16, :]
                total = total + taps[k] * jnp.where(depth >= k, moved, 0.0)
            half_ref[at : at + 16, lanes] = total.astype(BF16)
        return lost

    lost = lax.fori_loop(0, blocks, one_block, jnp.zeros((8, BLOCK_VOX), F32))
    loss_ref[...] = lost
    high = lost.astype(BF16).astype(F32)
    pair = jnp.concatenate([high, lost - high], axis=0)
    pad = jnp.zeros((16, rows - BLOCK_VOX), F32)
    pieces = 1 << len(orders[0])
    halves = pieces // 2
    send_ref[halves * width :, :] = jnp.concatenate([pair, pad], axis=1).astype(BF16)
    for p in range(halves):
        at = pl.multiple_of(picked(halves + p, orders) * width, width)
        send_ref[p * width : (p + 1) * width, :] = lax.dot_general(
            effective_ref[pl.ds(at, width), :], half_ref[...], NT, preferred_element_type=F32
        ).astype(BF16)


def rest_kernel(
    rows, orders, width, tm_bits, share, core_ref, effective_ref, half_ref, keep_ref, out_ref, own_ref, flipped
):
    halves = 1 << (len(orders[0]) - 1)
    flipped[...] = jnp.transpose(core_ref[MARGIN : MARGIN + rows, :])
    pieces = 1 << len(tm_bits)
    for q in reversed(range(pieces)):
        at = pl.multiple_of((lax.axis_index("tm") ^ block_at(q, tm_bits)) * share, share)
        part = jnp.dot(flipped[pl.ds(at, share), :], half_ref[...], preferred_element_type=F32)
        if q >= pieces // 2:
            slot = q - pieces // 2
            out_ref[slot * share : (slot + 1) * share, :] = part.astype(BF16)
        else:
            own_ref[q * share : (q + 1) * share, :] = part
    for p in range(halves):
        at = pl.multiple_of(picked(p, orders) * width, width)
        keep_ref[p * width : (p + 1) * width, :] = lax.dot_general(
            effective_ref[pl.ds(at, width), :], half_ref[...], NT, preferred_element_type=F32
        )


def slope_kernel(point_ref, depth_ref, slope_ref):
    act = lax.dot_general(
        point_ref[...], depth_ref[...], (((0,), (1,)), ((), ())), preferred_element_type=F32
    )
    slope_ref[...] = jax.vjp(jax.nn.gelu, act)[1](jnp.ones_like(act))[0]


def loss_pair(value, width):
    high = value.astype(BF16).astype(F32)
    pair = jnp.concatenate([high, value - high], axis=0)
    pad = jnp.zeros((16, width - BLOCK_VOX), F32)
    return jnp.concatenate([pair, pad], axis=1).astype(BF16)


def grad_kernel(keep_ref, arrived_ref, lost_ref, slope_ref, out_ref):
    width = keep_ref.shape[0]
    total = keep_ref[...] + arrived_ref[:width, :].astype(F32)
    out_ref[:width, :] = (total * slope_ref[...]).astype(BF16)
    pair = arrived_ref[width:, :BLOCK_VOX].astype(F32)
    out_ref[width:, :] = loss_pair(lost_ref[...] + pair[:8] + pair[8:], keep_ref.shape[1])


def early_kernel(parts, width, *refs):
    grad_refs, depth_refs, (total_ref,) = refs[:parts], refs[parts : 2 * parts], refs[2 * parts :]
    for col in range(0, total_ref.shape[1], 256):
        lanes = slice(col, col + 256)
        total = None
        for grad_ref, depth_ref in zip(grad_refs, depth_refs):
            part = jnp.dot(
                grad_ref[:width, :], depth_ref[:, lanes], preferred_element_type=F32
            )
            total = part if total is None else total + part
        total_ref[:, lanes] = total


def last_kernel(early, late, width, scale, total_ref, *refs):
    first_refs = refs[:early]
    grad_refs = refs[early : early + late]
    depth_refs = refs[early + late : early + 2 * late]
    point_ref, loss_ref = refs[early + 2 * late :]
    for col in range(0, total_ref.shape[1], 256):
        lanes = slice(col, col + 256)
        total = total_ref[:, lanes]
        for grad_ref, depth_ref in zip(grad_refs, depth_refs):
            total = total + jnp.dot(
                grad_ref[:width, :], depth_ref[:, lanes], preferred_element_type=F32
            )
        point_ref[lanes, :] = jnp.transpose(total)
    lost = None
    for ref in first_refs + grad_refs:
        part = ref[width:, :BLOCK_VOX].astype(F32)
        lost = part if lost is None else lost + part
    loss_ref[0, 0] = jnp.sum(lost) * scale


def readout_kernel(blocks, subject_ref, keep_ref, arrived_ref, gains_ref, out_ref):
    rows = [gains_ref[pl.ds(subject_ref[b], 1), :] for b in range(blocks)]
    rows += [rows[-1]] * (-blocks % 8)
    cols = jnp.transpose(jnp.concatenate(rows, axis=0))
    for b in range(blocks):
        lanes = slice(b * BLOCK_VOX, (b + 1) * BLOCK_VOX)
        total = keep_ref[:, lanes] + arrived_ref[:, lanes].astype(F32)
        out_ref[:, lanes] = total * cols[:, b : b + 1]


def shards(
    tm_count,
    vox_count,
    clip_features,
    depth_kernel,
    point_weight,
    session_lengths,
    subject_feature_gains,
    readout_weight,
    hrf_kernel,
    block_subject,
    block_live,
    bold_target,
):
    rows, feats = clip_features.shape
    slots = readout_weight.shape[1]
    blocks = slots // BLOCK_VOX
    subjects = subject_feature_gains.shape[0]
    width = feats // vox_count
    share = feats // tm_count
    vox_bits = list(range(vox_count.bit_length() - 1))
    orders = (vox_bits, [vox_bits[1], vox_bits[0]] + vox_bits[2:])
    tm_bits = list(range(tm_count.bit_length() - 1))

    def swap_tm(value, bit):
        return lax.ppermute(value, "tm", [(i, i ^ (1 << bit)) for i in range(tm_count)])

    def across(value, partner):
        pairs = []
        for t in range(tm_count):
            for v in range(vox_count):
                to = partner(t, v)
                if to is not None:
                    pairs.append((t * vox_count + v, to[0] * vox_count + to[1]))
        return lax.ppermute(value, ("tm", "vox"), pairs)

    def next_tm(t, v):
        other = t + 1 if t % 2 else t - 1
        return (other, v) if 0 <= other < tm_count else None

    def next_vox(t, v):
        if t % 2 == 0:
            return (t, v ^ 1)
        other = v + 1 if v % 2 else v - 1
        return (t, other) if 0 <= other < vox_count else None

    payload, ends = pl.pallas_call(
        functools.partial(pack_kernel, blocks),
        out_shape=(
            jax.ShapeDtypeStruct((4 * MARGIN, feats), BF16),
            jax.ShapeDtypeStruct((8, BLOCK_VOX), jnp.int32),
        ),
        grid=(1,),
        in_specs=[
            SMEM,
            SMEM,
            pl.BlockSpec((2 * MARGIN, feats), lambda i: (rows // (2 * MARGIN) - 1, 0)),
            pl.BlockSpec((MARGIN, feats), lambda i: (0, 0)),
            pl.BlockSpec((MARGIN, slots), lambda i: (0, 0)),
        ],
        out_specs=(VMEM, VMEM),
        cost_estimate=pl.CostEstimate(
            flops=int(6 * 1.15e9), bytes_accessed=1000000, transcendentals=0
        ),
    )(block_subject, block_live, clip_features, clip_features, bold_target)
    far = across(payload, next_tm)
    mine = across(ends, next_vox)
    near = swap_tm(payload, 0)

    depth_half, core_out = call(
        functools.partial(core_kernel, rows),
        (
            jax.ShapeDtypeStruct((rows, feats), BF16),
            jax.ShapeDtypeStruct((rows + 2 * MARGIN, feats), BF16),
        ),
        [
            (SMEM, session_lengths),
            (VMEM, clip_features),
            (VMEM, near),
            (VMEM, far),
            (VMEM, depth_kernel),
            (VMEM, point_weight),
        ],
        2.0,
        [
            pltpu.VMEM((rows + 3 * MARGIN, feats), BF16),
            pltpu.VMEM((rows + 2 * MARGIN, feats), BF16),
        ],
    )
    core_out, late_gains, mine = lax.optimization_barrier(
        (core_out, subject_feature_gains, mine)
    )
    twin = swap_tm(mine, 0)
    effective = call(
        functools.partial(gain_kernel, blocks),
        jax.ShapeDtypeStruct((feats, slots), BF16),
        [(SMEM, block_subject), (VMEM, late_gains), (VMEM, readout_weight)],
        1.5,
    )
    half, send, lost = call(
        functools.partial(voxel_kernel, rows, blocks, orders, width),
        (
            jax.ShapeDtypeStruct((rows, slots), BF16),
            jax.ShapeDtypeStruct((feats // 2 + 16, rows), BF16),
            jax.ShapeDtypeStruct((8, BLOCK_VOX), F32),
        ),
        [
            (SMEM, session_lengths),
            (SMEM, block_subject),
            (SMEM, block_live),
            (VMEM, mine),
            (VMEM, twin),
            (VMEM, core_out),
            (VMEM, effective),
            (VMEM, hrf_kernel),
            (VMEM, bold_target),
            (VMEM, near),
            (VMEM, far),
        ],
        5.0,
        [
            pltpu.VMEM((blocks, rows + 2 * MARGIN, BLOCK_VOX), F32),
            pltpu.VMEM((blocks, rows + MARGIN, BLOCK_VOX), F32),
            pltpu.VMEM((rows + MARGIN, slots), BF16),
            pltpu.VMEM((rows + MARGIN, BLOCK_VOX), jnp.int32),
            pltpu.VMEM((rows + MARGIN, BLOCK_VOX), jnp.int32),
            pltpu.VMEM((blocks, 16, BLOCK_VOX), F32),
        ],
    )
    keep, raw_send, raw_keep = call(
        functools.partial(rest_kernel, rows, orders, width, tm_bits, share),
        (
            jax.ShapeDtypeStruct((feats // 2, rows), F32),
            jax.ShapeDtypeStruct((feats // 2, slots), BF16),
            jax.ShapeDtypeStruct((feats // 2, slots), F32),
        ),
        [(VMEM, core_out), (VMEM, effective), (VMEM, half)],
        1.1,
        [pltpu.VMEM((feats, rows), BF16)],
    )

    def loss_rows(value):
        high = lax.reduce_precision(value, 8, 7)
        pair = jnp.concatenate([high, value - high], axis=0)
        return jnp.pad(pair, ((0, 0), (0, rows - BLOCK_VOX))).astype(BF16)

    def loss_of(arrived):
        pair = arrived[:, :BLOCK_VOX].astype(F32)
        return pair[:8] + pair[8:]

    col = lax.axis_index("vox") * width
    point_cols = lax.dynamic_slice_in_dim(point_weight, col, width, 1)
    slope = call(
        slope_kernel,
        jax.ShapeDtypeStruct((width, rows), F32),
        [(VMEM, point_cols), (VMEM, depth_half)],
        0.7,
    )
    own_gains = lax.dynamic_slice_in_dim(
        subject_feature_gains, lax.axis_index("tm") * share, share, 1
    )
    stages = len(vox_bits)
    paths = [()]
    for bit in reversed(tm_bits):
        paths = paths + [path + (bit,) for path in paths]
    depths = {(): depth_half}
    first = [(bit,) for bit in reversed(tm_bits)]
    for path in first:
        depths[path] = swap_tm(depth_half, path[0])
    raw_came = swap_tm(raw_send, tm_bits[0])
    for stage in range(stages):
        arrived = across(send, lambda t, v: (t, v ^ (1 << orders[t % 2][stage])))
        if stage == 0:
            held = lax.optimization_barrier((arrived, *[depths[path] for path in first]))
            arrived = held[0]
            depths.update(zip(first, held[1:]))
        if stage == min(1, stages - 1):
            for bit in tm_bits[1:]:
                raw_keep = raw_keep + raw_came.astype(F32)
                size = raw_keep.shape[0] // 2
                raw_send, raw_keep = raw_keep[size:].astype(BF16), raw_keep[:size]
                raw_came = swap_tm(raw_send, bit)
            arrived, raw_keep, slope, own_gains = lax.optimization_barrier(
                (arrived, raw_keep, slope, own_gains)
            )
        if stage + 1 < stages:
            size = keep.shape[0] // 2
            keep = keep + arrived[: 2 * size].astype(F32)
            lost = lost + loss_of(arrived[2 * size :])
            send = jnp.concatenate([keep[size:].astype(BF16), loss_rows(lost)], axis=0)
            keep = keep[:size]
    arrived, raw_came = lax.optimization_barrier((arrived, raw_came))
    for path in paths[1:]:
        if path not in depths:
            depths[path] = swap_tm(depths[path[:-1]], path[-1])
    pre_grad = call(
        grad_kernel,
        jax.ShapeDtypeStruct((width + 16, rows), BF16),
        [(VMEM, keep), (VMEM, arrived), (VMEM, lost), (VMEM, slope)],
        0.3,
    )
    grads = {(): pre_grad}
    for path in paths[1:]:
        grads[path] = swap_tm(grads[path[:-1]], path[-1])
    early = [(), (0,)]
    late = [path for path in paths if path not in early]
    total = call(
        functools.partial(early_kernel, len(early), width),
        jax.ShapeDtypeStruct((width, feats), F32),
        [(VMEM, grads[path]) for path in early] + [(VMEM, depths[path]) for path in early],
        0.8,
    )
    grad_readout = call(
        functools.partial(readout_kernel, blocks),
        jax.ShapeDtypeStruct((share, slots), F32),
        [(SMEM, block_subject), (VMEM, raw_keep), (VMEM, raw_came), (VMEM, own_gains)],
        0.8,
    )
    grad_point, loss_total = pl.pallas_call(
        functools.partial(
            last_kernel, len(early), len(late), width, 1.0 / (subjects * rows * tm_count)
        ),
        out_shape=(
            jax.ShapeDtypeStruct((feats, width), F32),
            jax.ShapeDtypeStruct((1, 1), F32),
        ),
        in_specs=[VMEM] * (1 + len(early) + 2 * len(late)),
        out_specs=(VMEM, SMEM),
        compiler_params=pltpu.CompilerParams(vmem_limit_bytes=16 << 20),
        cost_estimate=pl.CostEstimate(
            flops=int(1.15e9), bytes_accessed=1000000, transcendentals=0
        ),
    )(
        total,
        *[grads[path] for path in early],
        *[grads[path] for path in late],
        *[depths[path] for path in late],
    )
    return (loss_total.reshape(()), grad_readout, grad_point)


def solution(mesh):
    placed = (
        P("tm", None),
        P(),
        P(),
        P(),
        P(),
        P(None, "vox"),
        P(None, "vox"),
        P("vox"),
        P("vox"),
        P("tm", "vox"),
    )
    return jax.shard_map(
        functools.partial(shards, mesh.shape["tm"], mesh.shape["vox"]),
        mesh=mesh,
        in_specs=placed,
        out_specs=(P(), P("tm", "vox"), P(None, "vox")),
        check_vma=False,
    )
```

```python
import functools
import jax
import jax.numpy as jnp
from jax import lax
from jax.experimental import pallas as pl
from jax.experimental.pallas import tpu as pltpu
from jax.sharding import PartitionSpec as P

BLOCK_VOX = 128
KERNEL_TAPS = 3
TAP_SPACING = 8
HRF = 16
MARGIN = (KERNEL_TAPS - 1) * TAP_SPACING
F32 = jnp.float32
BF16 = jnp.bfloat16
NT = (((1,), (1,)), ((), ()))
VMEM = pl.BlockSpec(memory_space=pltpu.VMEM)
SMEM = pl.BlockSpec(memory_space=pltpu.SMEM)
HBM = pl.BlockSpec(memory_space=pltpu.HBM)


def call(body, outs, ins, micros, scratch=()):
    return pl.pallas_call(
        body,
        out_shape=outs,
        in_specs=[spec for spec, _ in ins],
        out_specs=jax.tree.map(lambda _: VMEM, outs),
        scratch_shapes=scratch,
        compiler_params=pltpu.CompilerParams(vmem_limit_bytes=16 << 20),
        cost_estimate=pl.CostEstimate(
            flops=int(micros * 1.15e9), bytes_accessed=int(micros * 1e6), transcendentals=0
        ),
    )(*[value for _, value in ins])


def session_starts(ends, time):
    start = jnp.zeros_like(time)
    for end in ends:
        start = jnp.where(time >= end, end, start)
    return start


def session_stops(ends, time):
    stop = jnp.zeros_like(time)
    for end in reversed(ends):
        stop = jnp.where(time < end, end, stop)
    return stop


def facts_of(ref, blocks):
    row = [ref[at : at + 1, :] for at in range(ref.shape[0])]
    return row[:blocks], row[blocks : 2 * blocks], row[2 * blocks :]


def pack_kernel(
    rows,
    blocks,
    subject_hbm,
    live_hbm,
    lengths_hbm,
    clip_ref,
    bold_ref,
    payload_ref,
    ends_ref,
    facts_ref,
    subject_ref,
    live_ref,
    lengths_ref,
    sems,
):
    slots = bold_ref.shape[1]
    tail = 2 * MARGIN
    moves = [
        (clip_ref.at[pl.ds(rows - tail, tail), :], payload_ref.at[pl.ds(0, tail), :]),
        (clip_ref.at[pl.ds(0, MARGIN), :], payload_ref.at[pl.ds(tail, MARGIN), :]),
        (
            bold_ref.at[pl.ds(0, MARGIN), :],
            payload_ref.at[pl.ds(tail + MARGIN, MARGIN), pl.ds(0, slots)],
        ),
        (subject_hbm, subject_ref),
        (live_hbm, live_ref),
        (lengths_hbm, lengths_ref),
    ]
    copies = [pltpu.make_async_copy(*move, sems.at[at]) for at, move in enumerate(moves)]
    for copy in copies:
        copy.start()
    payload_ref[3 * MARGIN :, slots:] = jnp.zeros_like(payload_ref[3 * MARGIN :, slots:])
    for copy in copies[3:]:
        copy.wait()
    row = lax.broadcasted_iota(jnp.int32, ends_ref.shape, 0)
    last = blocks - 1
    ends = jnp.where(row == 0, subject_ref[0], live_ref[0])
    ends = jnp.where(row == 2, subject_ref[last], ends)
    ends_ref[...] = jnp.where(row == 3, live_ref[last], ends)
    values = [subject_ref[b] for b in range(blocks)] + [live_ref[b] for b in range(blocks)]
    end = jnp.int32(0)
    for at in range(lengths_ref.shape[0]):
        end = end + lengths_ref[at]
        values.append(end)
    row = lax.broadcasted_iota(jnp.int32, facts_ref.shape, 0)
    facts = jnp.full(facts_ref.shape, end, jnp.int32)
    for at, value in enumerate(values):
        facts = jnp.where(row == at, value, facts)
    facts_ref[...] = facts
    for copy in copies[:3]:
        copy.wait()


def gain_kernel(blocks, facts_ref, gains_ref, weight_ref, core_ref, effective_ref, response_ref):
    slots = blocks * BLOCK_VOX
    subjects = gains_ref.shape[0]
    whole = gains_ref[...]
    high = whole.astype(BF16).astype(F32)
    middle = (whole - high).astype(BF16).astype(F32)
    low = whole - high - middle
    terms = jnp.concatenate([high, middle, low], axis=0).astype(BF16)
    owner = jnp.concatenate(facts_of(facts_ref, blocks)[0], axis=1)
    row = lax.broadcasted_iota(jnp.int32, (3 * subjects, slots), 0) % subjects
    pick = jnp.where(row == owner, 1.0, 0.0).astype(BF16)
    scale = lax.dot_general(
        terms, pick, (((0,), (0,)), ((), ())), preferred_element_type=F32
    )
    effective_ref[...] = (weight_ref[...].astype(F32) * scale).astype(BF16)
    for b in range(0, blocks, 2):
        many = min(2, blocks - b)
        lanes = slice(b * BLOCK_VOX, (b + many) * BLOCK_VOX)
        part = jnp.dot(core_ref[...], effective_ref[:, lanes], preferred_element_type=F32)
        part = part.astype(BF16).astype(F32)
        for c in range(many):
            response_ref[b + c] = part[:, c * BLOCK_VOX : (c + 1) * BLOCK_VOX]


def core_kernel(
    rows,
    blocks,
    facts_ref,
    clip_ref,
    near_ref,
    far_ref,
    taps_ref,
    point_ref,
    depth_ref,
    core_ref,
    ext,
    deep,
):
    feats = clip_ref.shape[1]
    odd = lax.axis_index("tm") % 2
    ext[2 * MARGIN : 2 * MARGIN + rows, :] = clip_ref[...]

    @pl.when(odd == 0)
    def _():
        ext[: 2 * MARGIN, :] = far_ref[: 2 * MARGIN, :]
        ext[2 * MARGIN + rows :, :] = near_ref[2 * MARGIN : 3 * MARGIN, :]

    @pl.when(odd == 1)
    def _():
        ext[: 2 * MARGIN, :] = near_ref[: 2 * MARGIN, :]
        ext[2 * MARGIN + rows :, :] = far_ref[2 * MARGIN : 3 * MARGIN, :]

    first = lax.axis_index("tm") * rows - MARGIN
    session_ends = facts_of(facts_ref, blocks)[2]
    taps = [taps_ref[k : k + 1, :] for k in range(KERNEL_TAPS)]
    for at in range(0, rows + 2 * MARGIN, 16):
        time = first + at + lax.broadcasted_iota(jnp.int32, (16, 128), 0)
        since = time - session_starts(session_ends, time)
        values = ext[at : at + 32, :].astype(F32)
        total = taps[0] * values[16:32]
        for k in range(1, KERNEL_TAPS):
            valid = (since >= k * TAP_SPACING).astype(F32)
            shift = MARGIN - k * TAP_SPACING
            moved = values[shift : shift + 16] * jnp.tile(valid, (1, feats // 128))
            total = total + taps[k] * moved
        deep[at : at + 16, :] = total.astype(BF16)
    depth_ref[...] = deep[MARGIN : MARGIN + rows, :]
    for col in range(0, feats, 256):
        lanes = slice(col, col + 256)
        act = jnp.dot(deep[...], point_ref[:, lanes], preferred_element_type=F32)
        core_ref[:, lanes] = (
            ext[MARGIN : MARGIN + rows + 2 * MARGIN, lanes].astype(F32) + jax.nn.gelu(act)
        ).astype(BF16)


def block_at(position, bits):
    return sum(
        ((position >> (len(bits) - 1 - s)) & 1) << bits[s] for s in range(len(bits))
    )


def picked(position, orders):
    even, odd = (block_at(position, bits) for bits in orders)
    mask = jnp.where(lax.axis_index("tm") % 2 == 0, even, odd)
    return lax.axis_index("vox") ^ mask


def spread_taps(hrf_ref, taps):
    for k in range(HRF):
        taps[k] = jnp.broadcast_to(hrf_ref[k : k + 1, :], taps.shape[1:])


def filtered(at, blocks, taps, limit, source, base, step):
    pairs = [(b, h) for b in range(blocks) for h in (0, 8)]
    depth = {h: limit[at + h : at + h + 8, :] for h in (0, 8)}
    total = {}
    for b, h in pairs:
        lanes = slice(b * BLOCK_VOX, (b + 1) * BLOCK_VOX)
        row = at + h + base
        total[b, h] = taps[0, :, lanes] * source[b, row : row + 8, :]
    for k in range(1, HRF):
        valid = {h: depth[h] >= k for h in (0, 8)}
        for b, h in pairs:
            lanes = slice(b * BLOCK_VOX, (b + 1) * BLOCK_VOX)
            row = at + h + base + step * k
            moved = jnp.where(valid[h], source[b, row : row + 8, :], 0.0)
            total[b, h] = total[b, h] + taps[k, :, lanes] * moved
    return total


def forward_kernel(
    rows, blocks, facts_ref, response_ref, hrf_ref, bold_ref, near_ref, far_ref, misfit_ref, bold, since, taps
):
    lead_rows = rows + MARGIN
    slots = blocks * BLOCK_VOX
    odd = lax.axis_index("tm") % 2
    bold[:rows, :] = bold_ref[...]

    @pl.when(odd == 0)
    def _():
        bold[rows:, :] = near_ref[3 * MARGIN :, :slots]

    @pl.when(odd == 1)
    def _():
        bold[rows:, :] = far_ref[3 * MARGIN :, :slots]

    first = lax.axis_index("tm") * rows
    time = first + lax.broadcasted_iota(jnp.int32, (lead_rows, BLOCK_VOX), 0)
    since[...] = time - session_starts(facts_of(facts_ref, blocks)[2], time)
    spread_taps(hrf_ref, taps)
    for at in range(0, lead_rows, 16):
        total = filtered(at, blocks, taps, since, response_ref, MARGIN, -1)
        for b in range(blocks):
            target = bold[at : at + 16, b * BLOCK_VOX : (b + 1) * BLOCK_VOX].astype(F32)
            for h in (0, 8):
                misfit_ref[b, at + h : at + h + 8, :] = total[b, h] - target[h : h + 8]


def backward_kernel(
    rows,
    blocks,
    orders,
    width,
    facts_ref,
    mine_ref,
    twin_ref,
    misfit_ref,
    effective_ref,
    hrf_ref,
    half_ref,
    send_ref,
    loss_ref,
    grads,
    left,
    taps,
):
    lead_rows = rows + MARGIN
    own_subjects, own_lives, session_ends = facts_of(facts_ref, blocks)
    first_core = lax.axis_index("tm") % 2 == 0
    low = jnp.where(first_core, mine_ref[...], twin_ref[...])
    high = jnp.where(first_core, twin_ref[...], mine_ref[...])
    even_vox = lax.axis_index("vox") % 2 == 0
    before = jnp.where(even_vox, high, low)
    after = jnp.where(even_vox, low, high)
    subjects = [before[2:3]] + own_subjects + [after[0:1]]
    lives = [before[3:4]] + own_lives + [after[1:2]]
    lane = lax.broadcasted_iota(jnp.int32, (8, BLOCK_VOX), 1)
    lost = jnp.zeros((8, BLOCK_VOX), F32)
    for b in range(blocks):
        count = lives[b + 1]
        count = count + jnp.where(subjects[b] == subjects[b + 1], lives[b], 0)
        count = count + jnp.where(subjects[b + 2] == subjects[b + 1], lives[b + 2], 0)
        inverse = 1.0 / jnp.maximum(count, 1).astype(F32)
        weight = jnp.where(lane < lives[b + 1], inverse, 0.0)
        double = 2.0 * weight
        for at in range(0, lead_rows, 8):
            misfit = misfit_ref[b, at : at + 8, :]
            grads[b, at : at + 8, :] = double * misfit
            if at < rows:
                lost = lost + weight * misfit * misfit
    loss_ref[...] = lost
    time = lax.axis_index("tm") * rows + lax.broadcasted_iota(jnp.int32, (rows, BLOCK_VOX), 0)
    left[...] = session_stops(session_ends, time) - 1 - time
    spread_taps(hrf_ref, taps)
    for at in range(0, rows, 16):
        total = filtered(at, blocks, taps, left, grads, 0, 1)
        for b in range(blocks):
            half_ref[at : at + 16, b * BLOCK_VOX : (b + 1) * BLOCK_VOX] = jnp.concatenate(
                [total[b, 0], total[b, 8]], axis=0
            ).astype(BF16)
    halves = 1 << (len(orders[0]) - 1)
    send_ref[halves * width :, :] = loss_pair(lost, rows)
    for p in range(halves):
        at = pl.multiple_of(picked(halves + p, orders) * width, width)
        send_ref[p * width : (p + 1) * width, :] = lax.dot_general(
            effective_ref[pl.ds(at, width), :], half_ref[...], NT, preferred_element_type=F32
        ).astype(BF16)


def rest_kernel(
    rows, orders, width, tm_bits, share, core_ref, effective_ref, half_ref, keep_ref, out_ref, own_ref, flipped
):
    halves = 1 << (len(orders[0]) - 1)
    flipped[...] = jnp.transpose(core_ref[MARGIN : MARGIN + rows, :])
    pieces = 1 << len(tm_bits)
    for q in reversed(range(pieces)):
        at = pl.multiple_of((lax.axis_index("tm") ^ block_at(q, tm_bits)) * share, share)
        part = jnp.dot(flipped[pl.ds(at, share), :], half_ref[...], preferred_element_type=F32)
        if q >= pieces // 2:
            slot = q - pieces // 2
            out_ref[slot * share : (slot + 1) * share, :] = part.astype(BF16)
        else:
            own_ref[q * share : (q + 1) * share, :] = part
    for p in range(halves):
        at = pl.multiple_of(picked(p, orders) * width, width)
        keep_ref[p * width : (p + 1) * width, :] = lax.dot_general(
            effective_ref[pl.ds(at, width), :], half_ref[...], NT, preferred_element_type=F32
        )


def slope_kernel(point_ref, depth_ref, slope_ref):
    act = lax.dot_general(
        point_ref[...], depth_ref[...], (((0,), (1,)), ((), ())), preferred_element_type=F32
    )
    slope_ref[...] = jax.vjp(jax.nn.gelu, act)[1](jnp.ones_like(act))[0]


def loss_pair(value, width):
    high = value.astype(BF16).astype(F32)
    pair = jnp.concatenate([high, value - high], axis=0)
    pad = jnp.zeros((16, width - BLOCK_VOX), F32)
    return jnp.concatenate([pair, pad], axis=1).astype(BF16)


def grad_kernel(keep_ref, arrived_ref, lost_ref, slope_ref, out_ref):
    width = keep_ref.shape[0]
    total = keep_ref[...] + arrived_ref[:width, :].astype(F32)
    out_ref[:width, :] = (total * slope_ref[...]).astype(BF16)
    pair = arrived_ref[width:, :BLOCK_VOX].astype(F32)
    out_ref[width:, :] = loss_pair(lost_ref[...] + pair[:8] + pair[8:], keep_ref.shape[1])


def early_kernel(parts, width, *refs):
    grad_refs, depth_refs, (total_ref,) = refs[:parts], refs[parts : 2 * parts], refs[2 * parts :]
    for col in range(0, total_ref.shape[1], 256):
        lanes = slice(col, col + 256)
        total = None
        for grad_ref, depth_ref in zip(grad_refs, depth_refs):
            part = jnp.dot(
                grad_ref[:width, :], depth_ref[:, lanes], preferred_element_type=F32
            )
            total = part if total is None else total + part
        total_ref[:, lanes] = total


def last_kernel(early, late, width, scale, total_ref, *refs):
    first_refs = refs[:early]
    grad_refs = refs[early : early + late]
    depth_refs = refs[early + late : early + 2 * late]
    point_ref, loss_ref = refs[early + 2 * late :]
    for col in range(0, total_ref.shape[1], 256):
        lanes = slice(col, col + 256)
        total = total_ref[:, lanes]
        for grad_ref, depth_ref in zip(grad_refs, depth_refs):
            total = total + jnp.dot(
                grad_ref[:width, :], depth_ref[:, lanes], preferred_element_type=F32
            )
        point_ref[lanes, :] = jnp.transpose(total)
    lost = None
    for ref in first_refs + grad_refs:
        part = ref[width:, :BLOCK_VOX].astype(F32)
        lost = part if lost is None else lost + part
    loss_ref[0, 0] = jnp.sum(lost) * scale


def readout_kernel(blocks, subject_ref, keep_ref, arrived_ref, gains_ref, out_ref):
    rows = [gains_ref[pl.ds(subject_ref[b], 1), :] for b in range(blocks)]
    rows += [rows[-1]] * (-blocks % 8)
    cols = jnp.transpose(jnp.concatenate(rows, axis=0))
    for b in range(blocks):
        lanes = slice(b * BLOCK_VOX, (b + 1) * BLOCK_VOX)
        total = keep_ref[:, lanes] + arrived_ref[:, lanes].astype(F32)
        out_ref[:, lanes] = total * cols[:, b : b + 1]


def shards(
    tm_count,
    vox_count,
    clip_features,
    depth_kernel,
    point_weight,
    session_lengths,
    subject_feature_gains,
    readout_weight,
    hrf_kernel,
    block_subject,
    block_live,
    bold_target,
):
    rows, feats = clip_features.shape
    slots = readout_weight.shape[1]
    blocks = slots // BLOCK_VOX
    subjects = subject_feature_gains.shape[0]
    width = feats // vox_count
    share = feats // tm_count
    vox_bits = list(range(vox_count.bit_length() - 1))
    orders = (vox_bits, [vox_bits[1], vox_bits[0]] + vox_bits[2:])
    tm_bits = list(range(tm_count.bit_length() - 1))

    def swap_tm(value, bit):
        return lax.ppermute(value, "tm", [(i, i ^ (1 << bit)) for i in range(tm_count)])

    def across(value, partner):
        pairs = []
        for t in range(tm_count):
            for v in range(vox_count):
                to = partner(t, v)
                if to is not None:
                    pairs.append((t * vox_count + v, to[0] * vox_count + to[1]))
        return lax.ppermute(value, ("tm", "vox"), pairs)

    def next_tm(t, v):
        other = t + 1 if t % 2 else t - 1
        return (other, v) if 0 <= other < tm_count else None

    def next_vox(t, v):
        if t % 2 == 0:
            return (t, v ^ 1)
        other = v + 1 if v % 2 else v - 1
        return (t, other) if 0 <= other < vox_count else None

    fact_rows = 2 * blocks + session_lengths.shape[0]
    fact_rows += -fact_rows % 8
    payload, ends, facts = pl.pallas_call(
        functools.partial(pack_kernel, rows, blocks),
        out_shape=(
            pltpu.VMEM((4 * MARGIN, feats), BF16),
            pltpu.VMEM((8, BLOCK_VOX), jnp.int32),
            pltpu.VMEM((fact_rows, BLOCK_VOX), jnp.int32),
        ),
        in_specs=[HBM] * 5,
        out_specs=(VMEM, VMEM, VMEM),
        scratch_shapes=[
            pltpu.SMEM((blocks,), jnp.int32),
            pltpu.SMEM((blocks,), jnp.int32),
            pltpu.SMEM(session_lengths.shape, jnp.int32),
            pltpu.SemaphoreType.DMA((6,)),
        ],
        cost_estimate=pl.CostEstimate(
            flops=int(6 * 1.15e9), bytes_accessed=1000000, transcendentals=0
        ),
    )(
        *[
            pltpu.with_memory_space_constraint(value, pltpu.HBM)
            for value in (block_subject, block_live, session_lengths, clip_features, bold_target)
        ]
    )
    far = across(payload, next_tm)
    mine = across(ends, next_vox)
    near = swap_tm(payload, 0)

    depth_half, core_out = call(
        functools.partial(core_kernel, rows, blocks),
        (
            jax.ShapeDtypeStruct((rows, feats), BF16),
            jax.ShapeDtypeStruct((rows + 2 * MARGIN, feats), BF16),
        ),
        [
            (VMEM, facts),
            (VMEM, clip_features),
            (VMEM, near),
            (VMEM, far),
            (VMEM, depth_kernel),
            (VMEM, point_weight),
        ],
        2.0,
        [
            pltpu.VMEM((rows + 3 * MARGIN, feats), BF16),
            pltpu.VMEM((rows + 2 * MARGIN, feats), BF16),
        ],
    )
    core_out, late_gains = lax.optimization_barrier((core_out, subject_feature_gains))
    effective, response = call(
        functools.partial(gain_kernel, blocks),
        (
            jax.ShapeDtypeStruct((feats, slots), BF16),
            jax.ShapeDtypeStruct((blocks, rows + 2 * MARGIN, BLOCK_VOX), F32),
        ),
        [(VMEM, facts), (VMEM, late_gains), (VMEM, readout_weight), (VMEM, core_out)],
        1.5,
    )
    response, mine = lax.optimization_barrier((response, mine))
    twin = swap_tm(mine, 0)
    misfit = call(
        functools.partial(forward_kernel, rows, blocks),
        jax.ShapeDtypeStruct((blocks, rows + MARGIN, BLOCK_VOX), F32),
        [
            (VMEM, facts),
            (VMEM, response),
            (VMEM, hrf_kernel),
            (VMEM, bold_target),
            (VMEM, near),
            (VMEM, far),
        ],
        1.5,
        [
            pltpu.VMEM((rows + MARGIN, slots), BF16),
            pltpu.VMEM((rows + MARGIN, BLOCK_VOX), jnp.int32),
            pltpu.VMEM((HRF, 8, slots), F32),
        ],
    )
    half, send, lost = call(
        functools.partial(backward_kernel, rows, blocks, orders, width),
        (
            jax.ShapeDtypeStruct((rows, slots), BF16),
            jax.ShapeDtypeStruct((feats // 2 + 16, rows), BF16),
            jax.ShapeDtypeStruct((8, BLOCK_VOX), F32),
        ),
        [
            (VMEM, facts),
            (VMEM, mine),
            (VMEM, twin),
            (VMEM, misfit),
            (VMEM, effective),
            (VMEM, hrf_kernel),
        ],
        2.5,
        [
            pltpu.VMEM((blocks, rows + MARGIN, BLOCK_VOX), F32),
            pltpu.VMEM((rows, BLOCK_VOX), jnp.int32),
            pltpu.VMEM((HRF, 8, slots), F32),
        ],
    )
    keep, raw_send, raw_keep = call(
        functools.partial(rest_kernel, rows, orders, width, tm_bits, share),
        (
            jax.ShapeDtypeStruct((feats // 2, rows), F32),
            jax.ShapeDtypeStruct((feats // 2, slots), BF16),
            jax.ShapeDtypeStruct((feats // 2, slots), F32),
        ),
        [(VMEM, core_out), (VMEM, effective), (VMEM, half)],
        1.1,
        [pltpu.VMEM((feats, rows), BF16)],
    )

    def loss_rows(value):
        high = lax.reduce_precision(value, 8, 7)
        pair = jnp.concatenate([high, value - high], axis=0)
        return jnp.pad(pair, ((0, 0), (0, rows - BLOCK_VOX))).astype(BF16)

    def loss_of(arrived):
        pair = arrived[:, :BLOCK_VOX].astype(F32)
        return pair[:8] + pair[8:]

    col = lax.axis_index("vox") * width
    point_cols = lax.dynamic_slice_in_dim(point_weight, col, width, 1)
    slope = call(
        slope_kernel,
        jax.ShapeDtypeStruct((width, rows), F32),
        [(VMEM, point_cols), (VMEM, depth_half)],
        0.7,
    )
    own_gains = lax.dynamic_slice_in_dim(
        subject_feature_gains, lax.axis_index("tm") * share, share, 1
    )
    stages = len(vox_bits)
    paths = [()]
    for bit in reversed(tm_bits):
        paths = paths + [path + (bit,) for path in paths]
    depths = {(): depth_half}
    first = [(bit,) for bit in reversed(tm_bits)]
    for path in first:
        depths[path] = swap_tm(depth_half, path[0])
    raw_came = swap_tm(raw_send, tm_bits[0])
    for stage in range(stages):
        arrived = across(send, lambda t, v: (t, v ^ (1 << orders[t % 2][stage])))
        if stage == 0:
            held = lax.optimization_barrier((arrived, *[depths[path] for path in first]))
            arrived = held[0]
            depths.update(zip(first, held[1:]))
        if stage == min(1, stages - 1):
            for bit in tm_bits[1:]:
                raw_keep = raw_keep + raw_came.astype(F32)
                size = raw_keep.shape[0] // 2
                raw_send, raw_keep = raw_keep[size:].astype(BF16), raw_keep[:size]
                raw_came = swap_tm(raw_send, bit)
            arrived, raw_keep, slope, own_gains = lax.optimization_barrier(
                (arrived, raw_keep, slope, own_gains)
            )
        if stage + 1 < stages:
            size = keep.shape[0] // 2
            keep = keep + arrived[: 2 * size].astype(F32)
            lost = lost + loss_of(arrived[2 * size :])
            send = jnp.concatenate([keep[size:].astype(BF16), loss_rows(lost)], axis=0)
            keep = keep[:size]
    arrived, raw_came = lax.optimization_barrier((arrived, raw_came))
    for path in paths[1:]:
        if path not in depths:
            depths[path] = swap_tm(depths[path[:-1]], path[-1])
    pre_grad = call(
        grad_kernel,
        jax.ShapeDtypeStruct((width + 16, rows), BF16),
        [(VMEM, keep), (VMEM, arrived), (VMEM, lost), (VMEM, slope)],
        0.3,
    )
    grads = {(): pre_grad}
    for path in paths[1:]:
        grads[path] = swap_tm(grads[path[:-1]], path[-1])
    early = [(), (0,)]
    late = [path for path in paths if path not in early]
    total = call(
        functools.partial(early_kernel, len(early), width),
        jax.ShapeDtypeStruct((width, feats), F32),
        [(VMEM, grads[path]) for path in early] + [(VMEM, depths[path]) for path in early],
        0.8,
    )
    grad_readout = call(
        functools.partial(readout_kernel, blocks),
        jax.ShapeDtypeStruct((share, slots), F32),
        [(SMEM, block_subject), (VMEM, raw_keep), (VMEM, raw_came), (VMEM, own_gains)],
        0.8,
    )
    grad_point, loss_total = pl.pallas_call(
        functools.partial(
            last_kernel, len(early), len(late), width, 1.0 / (subjects * rows * tm_count)
        ),
        out_shape=(
            jax.ShapeDtypeStruct((feats, width), F32),
            jax.ShapeDtypeStruct((1, 1), F32),
        ),
        in_specs=[VMEM] * (1 + len(early) + 2 * len(late)),
        out_specs=(VMEM, SMEM),
        compiler_params=pltpu.CompilerParams(vmem_limit_bytes=16 << 20),
        cost_estimate=pl.CostEstimate(
            flops=int(1.15e9), bytes_accessed=1000000, transcendentals=0
        ),
    )(
        total,
        *[grads[path] for path in early],
        *[grads[path] for path in late],
        *[depths[path] for path in late],
    )
    return (loss_total.reshape(()), grad_readout, grad_point)


def solution(mesh):
    placed = (
        P("tm", None),
        P(),
        P(),
        P(),
        P(),
        P(None, "vox"),
        P(None, "vox"),
        P("vox"),
        P("vox"),
        P("tm", "vox"),
    )
    return jax.shard_map(
        functools.partial(shards, mesh.shape["tm"], mesh.shape["vox"]),
        mesh=mesh,
        in_specs=placed,
        out_specs=(P(), P("tm", "vox"), P(None, "vox")),
        check_vma=False,
    )
```

```python
import functools
import jax
import jax.numpy as jnp
from jax import lax
from jax.experimental import pallas as pl
from jax.experimental.pallas import tpu as pltpu
from jax.sharding import PartitionSpec as P

BLOCK_VOX = 128
KERNEL_TAPS = 3
TAP_SPACING = 8
HRF = 16
MARGIN = (KERNEL_TAPS - 1) * TAP_SPACING
F32 = jnp.float32
BF16 = jnp.bfloat16
NT = (((1,), (1,)), ((), ()))
VMEM = pl.BlockSpec(memory_space=pltpu.VMEM)
SMEM = pl.BlockSpec(memory_space=pltpu.SMEM)
HBM = pl.BlockSpec(memory_space=pltpu.HBM)


def call(body, outs, ins, micros, scratch=()):
    return pl.pallas_call(
        body,
        out_shape=outs,
        in_specs=[spec for spec, _ in ins],
        out_specs=jax.tree.map(lambda _: VMEM, outs),
        scratch_shapes=scratch,
        compiler_params=pltpu.CompilerParams(vmem_limit_bytes=16 << 20),
        cost_estimate=pl.CostEstimate(
            flops=int(micros * 1.15e9), bytes_accessed=int(micros * 1e6), transcendentals=0
        ),
    )(*[value for _, value in ins])


def session_starts(ends, time):
    start = jnp.zeros_like(time)
    for end in ends:
        start = jnp.where(time >= end, end, start)
    return start


def session_stops(ends, time):
    stop = jnp.zeros_like(time)
    for end in reversed(ends):
        stop = jnp.where(time < end, end, stop)
    return stop


def facts_of(ref, blocks):
    row = [ref[at : at + 1, :] for at in range(ref.shape[0])]
    return row[:blocks], row[blocks : 2 * blocks], row[2 * blocks :]


def pack_kernel(
    rows,
    blocks,
    subject_hbm,
    live_hbm,
    lengths_hbm,
    clip_ref,
    bold_ref,
    payload_ref,
    ends_ref,
    facts_ref,
    subject_ref,
    live_ref,
    lengths_ref,
    sems,
):
    slots = bold_ref.shape[1]
    tail = 2 * MARGIN
    moves = [
        (clip_ref.at[pl.ds(rows - tail, tail), :], payload_ref.at[pl.ds(0, tail), :]),
        (clip_ref.at[pl.ds(0, MARGIN), :], payload_ref.at[pl.ds(tail, MARGIN), :]),
        (
            bold_ref.at[pl.ds(0, MARGIN), :],
            payload_ref.at[pl.ds(tail + MARGIN, MARGIN), pl.ds(0, slots)],
        ),
        (subject_hbm, subject_ref),
        (live_hbm, live_ref),
        (lengths_hbm, lengths_ref),
    ]
    copies = [pltpu.make_async_copy(*move, sems.at[at]) for at, move in enumerate(moves)]
    for copy in copies:
        copy.start()
    payload_ref[3 * MARGIN :, slots:] = jnp.zeros_like(payload_ref[3 * MARGIN :, slots:])
    for copy in copies[3:]:
        copy.wait()
    row = lax.broadcasted_iota(jnp.int32, ends_ref.shape, 0)
    last = blocks - 1
    ends = jnp.where(row == 0, subject_ref[0], live_ref[0])
    ends = jnp.where(row == 2, subject_ref[last], ends)
    ends_ref[...] = jnp.where(row == 3, live_ref[last], ends)
    values = [subject_ref[b] for b in range(blocks)] + [live_ref[b] for b in range(blocks)]
    end = jnp.int32(0)
    for at in range(lengths_ref.shape[0]):
        end = end + lengths_ref[at]
        values.append(end)
    row = lax.broadcasted_iota(jnp.int32, facts_ref.shape, 0)
    facts = jnp.full(facts_ref.shape, end, jnp.int32)
    for at, value in enumerate(values):
        facts = jnp.where(row == at, value, facts)
    facts_ref[...] = facts
    for copy in copies[:3]:
        copy.wait()


def gain_kernel(blocks, facts_ref, gains_ref, weight_ref, core_ref, effective_ref, response_ref):
    slots = blocks * BLOCK_VOX
    subjects = gains_ref.shape[0]
    whole = gains_ref[...]
    high = whole.astype(BF16).astype(F32)
    middle = (whole - high).astype(BF16).astype(F32)
    low = whole - high - middle
    terms = jnp.concatenate([high, middle, low], axis=0).astype(BF16)
    owner = jnp.concatenate(facts_of(facts_ref, blocks)[0], axis=1)
    row = lax.broadcasted_iota(jnp.int32, (3 * subjects, slots), 0) % subjects
    pick = jnp.where(row == owner, 1.0, 0.0).astype(BF16)
    scale = lax.dot_general(
        terms, pick, (((0,), (0,)), ((), ())), preferred_element_type=F32
    )
    effective_ref[...] = (weight_ref[...].astype(F32) * scale).astype(BF16)
    for b in range(0, blocks, 2):
        many = min(2, blocks - b)
        lanes = slice(b * BLOCK_VOX, (b + many) * BLOCK_VOX)
        part = jnp.dot(core_ref[...], effective_ref[:, lanes], preferred_element_type=F32)
        part = part.astype(BF16).astype(F32)
        for c in range(many):
            response_ref[b + c] = part[:, c * BLOCK_VOX : (c + 1) * BLOCK_VOX]


def conv_kernel(
    rows, blocks, facts_ref, clip_ref, near_ref, far_ref, taps_ref, depth_ref, deep_ref, ext
):
    feats = clip_ref.shape[1]
    odd = lax.axis_index("tm") % 2
    ext[2 * MARGIN : 2 * MARGIN + rows, :] = clip_ref[...]

    @pl.when(odd == 0)
    def _():
        ext[: 2 * MARGIN, :] = far_ref[: 2 * MARGIN, :]
        ext[2 * MARGIN + rows :, :] = near_ref[2 * MARGIN : 3 * MARGIN, :]

    @pl.when(odd == 1)
    def _():
        ext[: 2 * MARGIN, :] = near_ref[: 2 * MARGIN, :]
        ext[2 * MARGIN + rows :, :] = far_ref[2 * MARGIN : 3 * MARGIN, :]

    first = lax.axis_index("tm") * rows - MARGIN
    session_ends = facts_of(facts_ref, blocks)[2]
    taps = [taps_ref[k : k + 1, :] for k in range(KERNEL_TAPS)]
    for at in range(0, rows + 2 * MARGIN, 16):
        time = first + at + lax.broadcasted_iota(jnp.int32, (16, 128), 0)
        since = time - session_starts(session_ends, time)
        values = ext[at : at + 32, :].astype(F32)
        total = taps[0] * values[16:32]
        for k in range(1, KERNEL_TAPS):
            valid = (since >= k * TAP_SPACING).astype(F32)
            shift = MARGIN - k * TAP_SPACING
            moved = values[shift : shift + 16] * jnp.tile(valid, (1, feats // 128))
            total = total + taps[k] * moved
        deep_ref[at : at + 16, :] = total.astype(BF16)
    depth_ref[...] = deep_ref[MARGIN : MARGIN + rows, :]


def core_kernel(rows, clip_ref, near_ref, far_ref, deep_ref, point_ref, core_ref, ext):
    feats = clip_ref.shape[1]
    odd = lax.axis_index("tm") % 2
    ext[MARGIN : MARGIN + rows, :] = clip_ref[...]

    @pl.when(odd == 0)
    def _():
        ext[:MARGIN, :] = far_ref[MARGIN : 2 * MARGIN, :]
        ext[MARGIN + rows :, :] = near_ref[2 * MARGIN : 3 * MARGIN, :]

    @pl.when(odd == 1)
    def _():
        ext[:MARGIN, :] = near_ref[MARGIN : 2 * MARGIN, :]
        ext[MARGIN + rows :, :] = far_ref[2 * MARGIN : 3 * MARGIN, :]

    for col in range(0, feats, 256):
        lanes = slice(col, col + 256)
        act = jnp.dot(deep_ref[...], point_ref[:, lanes], preferred_element_type=F32)
        core_ref[:, lanes] = (ext[:, lanes].astype(F32) + jax.nn.gelu(act)).astype(BF16)


def block_at(position, bits):
    return sum(
        ((position >> (len(bits) - 1 - s)) & 1) << bits[s] for s in range(len(bits))
    )


def picked(position, orders):
    even, odd = (block_at(position, bits) for bits in orders)
    mask = jnp.where(lax.axis_index("tm") % 2 == 0, even, odd)
    return lax.axis_index("vox") ^ mask


def spread_taps(hrf_ref, taps):
    for k in range(HRF):
        taps[k] = jnp.broadcast_to(hrf_ref[k : k + 1, :], taps.shape[1:])


def filtered(at, blocks, taps, limit, source, base, step):
    pairs = [(b, h) for b in range(blocks) for h in (0, 8)]
    depth = {h: limit[at + h : at + h + 8, :] for h in (0, 8)}
    total = {}
    for b, h in pairs:
        lanes = slice(b * BLOCK_VOX, (b + 1) * BLOCK_VOX)
        row = at + h + base
        total[b, h] = taps[0, :, lanes] * source[b, row : row + 8, :]
    for k in range(1, HRF):
        valid = {h: depth[h] >= k for h in (0, 8)}
        for b, h in pairs:
            lanes = slice(b * BLOCK_VOX, (b + 1) * BLOCK_VOX)
            row = at + h + base + step * k
            moved = jnp.where(valid[h], source[b, row : row + 8, :], 0.0)
            total[b, h] = total[b, h] + taps[k, :, lanes] * moved
    return total


def forward_kernel(
    rows, blocks, facts_ref, response_ref, hrf_ref, bold_ref, near_ref, far_ref, misfit_ref, bold, since, taps
):
    lead_rows = rows + MARGIN
    slots = blocks * BLOCK_VOX
    odd = lax.axis_index("tm") % 2
    bold[:rows, :] = bold_ref[...]

    @pl.when(odd == 0)
    def _():
        bold[rows:, :] = near_ref[3 * MARGIN :, :slots]

    @pl.when(odd == 1)
    def _():
        bold[rows:, :] = far_ref[3 * MARGIN :, :slots]

    first = lax.axis_index("tm") * rows
    time = first + lax.broadcasted_iota(jnp.int32, (lead_rows, BLOCK_VOX), 0)
    since[...] = time - session_starts(facts_of(facts_ref, blocks)[2], time)
    spread_taps(hrf_ref, taps)
    for at in range(0, lead_rows, 16):
        total = filtered(at, blocks, taps, since, response_ref, MARGIN, -1)
        for b in range(blocks):
            target = bold[at : at + 16, b * BLOCK_VOX : (b + 1) * BLOCK_VOX].astype(F32)
            for h in (0, 8):
                misfit_ref[b, at + h : at + h + 8, :] = total[b, h] - target[h : h + 8]


def backward_kernel(
    rows,
    blocks,
    orders,
    width,
    facts_ref,
    mine_ref,
    twin_ref,
    misfit_ref,
    effective_ref,
    hrf_ref,
    half_ref,
    send_ref,
    loss_ref,
    grads,
    left,
    taps,
):
    lead_rows = rows + MARGIN
    own_subjects, own_lives, session_ends = facts_of(facts_ref, blocks)
    first_core = lax.axis_index("tm") % 2 == 0
    low = jnp.where(first_core, mine_ref[...], twin_ref[...])
    high = jnp.where(first_core, twin_ref[...], mine_ref[...])
    even_vox = lax.axis_index("vox") % 2 == 0
    before = jnp.where(even_vox, high, low)
    after = jnp.where(even_vox, low, high)
    subjects = [before[2:3]] + own_subjects + [after[0:1]]
    lives = [before[3:4]] + own_lives + [after[1:2]]
    lane = lax.broadcasted_iota(jnp.int32, (8, BLOCK_VOX), 1)
    lost = jnp.zeros((8, BLOCK_VOX), F32)
    for b in range(blocks):
        count = lives[b + 1]
        count = count + jnp.where(subjects[b] == subjects[b + 1], lives[b], 0)
        count = count + jnp.where(subjects[b + 2] == subjects[b + 1], lives[b + 2], 0)
        inverse = 1.0 / jnp.maximum(count, 1).astype(F32)
        weight = jnp.where(lane < lives[b + 1], inverse, 0.0)
        double = 2.0 * weight
        for at in range(0, lead_rows, 8):
            misfit = misfit_ref[b, at : at + 8, :]
            grads[b, at : at + 8, :] = double * misfit
            if at < rows:
                lost = lost + weight * misfit * misfit
    loss_ref[...] = lost
    time = lax.axis_index("tm") * rows + lax.broadcasted_iota(jnp.int32, (rows, BLOCK_VOX), 0)
    left[...] = session_stops(session_ends, time) - 1 - time
    spread_taps(hrf_ref, taps)
    for at in range(0, rows, 16):
        total = filtered(at, blocks, taps, left, grads, 0, 1)
        for b in range(blocks):
            half_ref[at : at + 16, b * BLOCK_VOX : (b + 1) * BLOCK_VOX] = jnp.concatenate(
                [total[b, 0], total[b, 8]], axis=0
            ).astype(BF16)
    halves = 1 << (len(orders[0]) - 1)
    send_ref[halves * width :, :] = loss_pair(lost, rows)
    for p in range(halves):
        at = pl.multiple_of(picked(halves + p, orders) * width, width)
        send_ref[p * width : (p + 1) * width, :] = lax.dot_general(
            effective_ref[pl.ds(at, width), :], half_ref[...], NT, preferred_element_type=F32
        ).astype(BF16)


def rest_kernel(
    rows, orders, width, tm_bits, share, core_ref, effective_ref, half_ref, keep_ref, out_ref, own_ref, flipped
):
    halves = 1 << (len(orders[0]) - 1)
    flipped[...] = jnp.transpose(core_ref[MARGIN : MARGIN + rows, :])
    pieces = 1 << len(tm_bits)
    for q in reversed(range(pieces)):
        at = pl.multiple_of((lax.axis_index("tm") ^ block_at(q, tm_bits)) * share, share)
        part = jnp.dot(flipped[pl.ds(at, share), :], half_ref[...], preferred_element_type=F32)
        if q >= pieces // 2:
            slot = q - pieces // 2
            out_ref[slot * share : (slot + 1) * share, :] = part.astype(BF16)
        else:
            own_ref[q * share : (q + 1) * share, :] = part
    for p in range(halves):
        at = pl.multiple_of(picked(p, orders) * width, width)
        keep_ref[p * width : (p + 1) * width, :] = lax.dot_general(
            effective_ref[pl.ds(at, width), :], half_ref[...], NT, preferred_element_type=F32
        )


def slope_kernel(point_ref, depth_ref, slope_ref):
    act = lax.dot_general(
        point_ref[...], depth_ref[...], (((0,), (1,)), ((), ())), preferred_element_type=F32
    )
    slope_ref[...] = jax.vjp(jax.nn.gelu, act)[1](jnp.ones_like(act))[0]


def loss_pair(value, width):
    high = value.astype(BF16).astype(F32)
    pair = jnp.concatenate([high, value - high], axis=0)
    pad = jnp.zeros((16, width - BLOCK_VOX), F32)
    return jnp.concatenate([pair, pad], axis=1).astype(BF16)


def grad_kernel(keep_ref, arrived_ref, lost_ref, slope_ref, out_ref):
    width = keep_ref.shape[0]
    total = keep_ref[...] + arrived_ref[:width, :].astype(F32)
    out_ref[:width, :] = (total * slope_ref[...]).astype(BF16)
    pair = arrived_ref[width:, :BLOCK_VOX].astype(F32)
    out_ref[width:, :] = loss_pair(lost_ref[...] + pair[:8] + pair[8:], keep_ref.shape[1])


def early_kernel(parts, width, *refs):
    grad_refs, depth_refs, (total_ref,) = refs[:parts], refs[parts : 2 * parts], refs[2 * parts :]
    for col in range(0, total_ref.shape[1], 256):
        lanes = slice(col, col + 256)
        total = None
        for grad_ref, depth_ref in zip(grad_refs, depth_refs):
            part = jnp.dot(
                grad_ref[:width, :], depth_ref[:, lanes], preferred_element_type=F32
            )
            total = part if total is None else total + part
        total_ref[:, lanes] = total


def later_kernel(parts, width, before_ref, *refs):
    grad_refs, depth_refs, (total_ref,) = refs[:parts], refs[parts : 2 * parts], refs[2 * parts :]
    for col in range(0, total_ref.shape[1], 256):
        lanes = slice(col, col + 256)
        total = before_ref[:, lanes]
        for grad_ref, depth_ref in zip(grad_refs, depth_refs):
            total = total + jnp.dot(
                grad_ref[:width, :], depth_ref[:, lanes], preferred_element_type=F32
            )
        total_ref[:, lanes] = total


def last_kernel(others, parts, width, scale, total_ref, *refs):
    other_refs = refs[:others]
    grad_refs = refs[others : others + parts]
    depth_refs = refs[others + parts : others + 2 * parts]
    point_ref, loss_ref = refs[others + 2 * parts :]
    lost = None
    for ref in other_refs + grad_refs:
        part = ref[width:, :BLOCK_VOX].astype(F32)
        lost = part if lost is None else lost + part
    loss_ref[0, 0] = jnp.sum(lost) * scale
    for col in range(0, total_ref.shape[1], 256):
        lanes = slice(col, col + 256)
        total = total_ref[:, lanes]
        for grad_ref, depth_ref in zip(grad_refs, depth_refs):
            total = total + jnp.dot(
                grad_ref[:width, :], depth_ref[:, lanes], preferred_element_type=F32
            )
        point_ref[lanes, :] = jnp.transpose(total)


def readout_kernel(blocks, subject_ref, keep_ref, arrived_ref, gains_ref, out_ref):
    rows = [gains_ref[pl.ds(subject_ref[b], 1), :] for b in range(blocks)]
    rows += [rows[-1]] * (-blocks % 8)
    cols = jnp.transpose(jnp.concatenate(rows, axis=0))
    for b in range(blocks):
        lanes = slice(b * BLOCK_VOX, (b + 1) * BLOCK_VOX)
        total = keep_ref[:, lanes] + arrived_ref[:, lanes].astype(F32)
        out_ref[:, lanes] = total * cols[:, b : b + 1]


def shards(
    tm_count,
    vox_count,
    clip_features,
    depth_kernel,
    point_weight,
    session_lengths,
    subject_feature_gains,
    readout_weight,
    hrf_kernel,
    block_subject,
    block_live,
    bold_target,
):
    rows, feats = clip_features.shape
    slots = readout_weight.shape[1]
    blocks = slots // BLOCK_VOX
    subjects = subject_feature_gains.shape[0]
    width = feats // vox_count
    share = feats // tm_count
    vox_bits = list(range(vox_count.bit_length() - 1))
    orders = (vox_bits, [vox_bits[1], vox_bits[0]] + vox_bits[2:])
    tm_bits = list(range(tm_count.bit_length() - 1))

    def swap_tm(value, bit):
        return lax.ppermute(value, "tm", [(i, i ^ (1 << bit)) for i in range(tm_count)])

    def across(value, partner):
        pairs = []
        for t in range(tm_count):
            for v in range(vox_count):
                to = partner(t, v)
                if to is not None:
                    pairs.append((t * vox_count + v, to[0] * vox_count + to[1]))
        return lax.ppermute(value, ("tm", "vox"), pairs)

    def next_tm(t, v):
        other = t + 1 if t % 2 else t - 1
        return (other, v) if 0 <= other < tm_count else None

    def next_vox(t, v):
        if t % 2 == 0:
            return (t, v ^ 1)
        other = v + 1 if v % 2 else v - 1
        return (t, other) if 0 <= other < vox_count else None

    fact_rows = 2 * blocks + session_lengths.shape[0]
    fact_rows += -fact_rows % 8
    payload, ends, facts = pl.pallas_call(
        functools.partial(pack_kernel, rows, blocks),
        out_shape=(
            pltpu.VMEM((4 * MARGIN, feats), BF16),
            pltpu.VMEM((8, BLOCK_VOX), jnp.int32),
            pltpu.VMEM((fact_rows, BLOCK_VOX), jnp.int32),
        ),
        in_specs=[HBM] * 5,
        out_specs=(VMEM, VMEM, VMEM),
        scratch_shapes=[
            pltpu.SMEM((blocks,), jnp.int32),
            pltpu.SMEM((blocks,), jnp.int32),
            pltpu.SMEM(session_lengths.shape, jnp.int32),
            pltpu.SemaphoreType.DMA((6,)),
        ],
        cost_estimate=pl.CostEstimate(
            flops=int(6 * 1.15e9), bytes_accessed=1000000, transcendentals=0
        ),
    )(
        *[
            pltpu.with_memory_space_constraint(value, pltpu.HBM)
            for value in (block_subject, block_live, session_lengths, clip_features, bold_target)
        ]
    )
    far = across(payload, next_tm)
    mine = across(ends, next_vox)
    near = swap_tm(payload, 0)

    halos = [(VMEM, clip_features), (VMEM, near), (VMEM, far)]
    depth_half, deep = call(
        functools.partial(conv_kernel, rows, blocks),
        (
            jax.ShapeDtypeStruct((rows, feats), BF16),
            jax.ShapeDtypeStruct((rows + 2 * MARGIN, feats), BF16),
        ),
        [(VMEM, facts)] + halos + [(VMEM, depth_kernel)],
        0.6,
        [pltpu.VMEM((rows + 3 * MARGIN, feats), BF16)],
    )
    core_out = call(
        functools.partial(core_kernel, rows),
        jax.ShapeDtypeStruct((rows + 2 * MARGIN, feats), BF16),
        halos + [(VMEM, deep), (VMEM, point_weight)],
        1.0,
        [pltpu.VMEM((rows + 2 * MARGIN, feats), BF16)],
    )
    core_out, late_gains = lax.optimization_barrier((core_out, subject_feature_gains))
    effective, response = call(
        functools.partial(gain_kernel, blocks),
        (
            jax.ShapeDtypeStruct((feats, slots), BF16),
            jax.ShapeDtypeStruct((blocks, rows + 2 * MARGIN, BLOCK_VOX), F32),
        ),
        [(VMEM, facts), (VMEM, late_gains), (VMEM, readout_weight), (VMEM, core_out)],
        1.5,
    )
    response, mine = lax.optimization_barrier((response, mine))
    twin = swap_tm(mine, 0)
    misfit = call(
        functools.partial(forward_kernel, rows, blocks),
        jax.ShapeDtypeStruct((blocks, rows + MARGIN, BLOCK_VOX), F32),
        [
            (VMEM, facts),
            (VMEM, response),
            (VMEM, hrf_kernel),
            (VMEM, bold_target),
            (VMEM, near),
            (VMEM, far),
        ],
        1.5,
        [
            pltpu.VMEM((rows + MARGIN, slots), BF16),
            pltpu.VMEM((rows + MARGIN, BLOCK_VOX), jnp.int32),
            pltpu.VMEM((HRF, 8, slots), F32),
        ],
    )
    half, send, lost = call(
        functools.partial(backward_kernel, rows, blocks, orders, width),
        (
            jax.ShapeDtypeStruct((rows, slots), BF16),
            jax.ShapeDtypeStruct((feats // 2 + 16, rows), BF16),
            jax.ShapeDtypeStruct((8, BLOCK_VOX), F32),
        ),
        [
            (VMEM, facts),
            (VMEM, mine),
            (VMEM, twin),
            (VMEM, misfit),
            (VMEM, effective),
            (VMEM, hrf_kernel),
        ],
        2.5,
        [
            pltpu.VMEM((blocks, rows + MARGIN, BLOCK_VOX), F32),
            pltpu.VMEM((rows, BLOCK_VOX), jnp.int32),
            pltpu.VMEM((HRF, 8, slots), F32),
        ],
    )
    keep, raw_send, raw_keep = call(
        functools.partial(rest_kernel, rows, orders, width, tm_bits, share),
        (
            jax.ShapeDtypeStruct((feats // 2, rows), F32),
            jax.ShapeDtypeStruct((feats // 2, slots), BF16),
            jax.ShapeDtypeStruct((feats // 2, slots), F32),
        ),
        [(VMEM, core_out), (VMEM, effective), (VMEM, half)],
        1.1,
        [pltpu.VMEM((feats, rows), BF16)],
    )

    def loss_rows(value):
        high = lax.reduce_precision(value, 8, 7)
        pair = jnp.concatenate([high, value - high], axis=0)
        return jnp.pad(pair, ((0, 0), (0, rows - BLOCK_VOX))).astype(BF16)

    def loss_of(arrived):
        pair = arrived[:, :BLOCK_VOX].astype(F32)
        return pair[:8] + pair[8:]

    col = lax.axis_index("vox") * width
    point_cols = lax.dynamic_slice_in_dim(point_weight, col, width, 1)
    slope = call(
        slope_kernel,
        jax.ShapeDtypeStruct((width, rows), F32),
        [(VMEM, point_cols), (VMEM, depth_half)],
        0.7,
    )
    own_gains = lax.dynamic_slice_in_dim(
        subject_feature_gains, lax.axis_index("tm") * share, share, 1
    )
    stages = len(vox_bits)
    paths = [()]
    for bit in reversed(tm_bits):
        paths = paths + [path + (bit,) for path in paths]
    depths = {(): depth_half}
    first = [(bit,) for bit in reversed(tm_bits)]
    for path in first:
        depths[path] = swap_tm(depth_half, path[0])
    raw_came = swap_tm(raw_send, tm_bits[0])
    for stage in range(stages):
        arrived = across(send, lambda t, v: (t, v ^ (1 << orders[t % 2][stage])))
        if stage == 0:
            held = lax.optimization_barrier((arrived, *[depths[path] for path in first]))
            arrived = held[0]
            depths.update(zip(first, held[1:]))
        if stage == min(1, stages - 1):
            for bit in tm_bits[1:]:
                raw_keep = raw_keep + raw_came.astype(F32)
                size = raw_keep.shape[0] // 2
                raw_send, raw_keep = raw_keep[size:].astype(BF16), raw_keep[:size]
                raw_came = swap_tm(raw_send, bit)
            arrived, raw_keep, slope, own_gains = lax.optimization_barrier(
                (arrived, raw_keep, slope, own_gains)
            )
        if stage + 1 < stages:
            size = keep.shape[0] // 2
            keep = keep + arrived[: 2 * size].astype(F32)
            lost = lost + loss_of(arrived[2 * size :])
            send = jnp.concatenate([keep[size:].astype(BF16), loss_rows(lost)], axis=0)
            keep = keep[:size]
    arrived, raw_came = lax.optimization_barrier((arrived, raw_came))
    for path in paths[1:]:
        if path not in depths:
            depths[path] = swap_tm(depths[path[:-1]], path[-1])
    pre_grad = call(
        grad_kernel,
        jax.ShapeDtypeStruct((width + 16, rows), BF16),
        [(VMEM, keep), (VMEM, arrived), (VMEM, lost), (VMEM, slope)],
        0.3,
    )
    groups = [[(), (0,)], [path for path in paths[1:] if path[-1] != 0]]
    groups.append([path for path in paths if path not in groups[0] + groups[1]])

    def operands(group):
        return [(VMEM, grads[path]) for path in group] + [(VMEM, depths[path]) for path in group]

    grads = {(): pre_grad}
    for path in groups[0][1:] + groups[1]:
        grads[path] = swap_tm(grads[path[:-1]], path[-1])
    total_shape = jax.ShapeDtypeStruct((width, feats), F32)
    total = call(
        functools.partial(early_kernel, len(groups[0]), width), total_shape, operands(groups[0]), 0.3
    )
    top = groups[1][-1]
    grad_readout = call(
        functools.partial(readout_kernel, blocks),
        jax.ShapeDtypeStruct((share, slots), F32),
        [(SMEM, block_subject), (VMEM, raw_keep), (VMEM, raw_came), (VMEM, own_gains)],
        0.8,
    )
    grads[top], total, grad_readout = lax.optimization_barrier(
        (grads[top], total, grad_readout)
    )
    for path in groups[2]:
        grads[path] = swap_tm(grads[path[:-1]], path[-1])
    total = call(
        functools.partial(later_kernel, len(groups[1]), width),
        total_shape,
        [(VMEM, total)] + operands(groups[1]),
        0.3,
    )
    others = groups[0] + groups[1]
    ins = [(VMEM, total)] + [(VMEM, grads[path]) for path in others] + operands(groups[2])
    grad_point, loss_total = pl.pallas_call(
        functools.partial(
            last_kernel, len(others), len(groups[2]), width, 1.0 / (subjects * rows * tm_count)
        ),
        out_shape=(
            jax.ShapeDtypeStruct((feats, width), F32),
            jax.ShapeDtypeStruct((1, 1), F32),
        ),
        in_specs=[spec for spec, _ in ins],
        out_specs=(VMEM, SMEM),
        compiler_params=pltpu.CompilerParams(vmem_limit_bytes=16 << 20),
        cost_estimate=pl.CostEstimate(
            flops=int(1.15e9), bytes_accessed=1000000, transcendentals=0
        ),
    )(*[value for _, value in ins])
    return (loss_total.reshape(()), grad_readout, grad_point)


def solution(mesh):
    placed = (
        P("tm", None),
        P(),
        P(),
        P(),
        P(),
        P(None, "vox"),
        P(None, "vox"),
        P("vox"),
        P("vox"),
        P("tm", "vox"),
    )
    return jax.shard_map(
        functools.partial(shards, mesh.shape["tm"], mesh.shape["vox"]),
        mesh=mesh,
        in_specs=placed,
        out_specs=(P(), P("tm", "vox"), P(None, "vox")),
        check_vma=False,
    )
```

```python
import functools
import jax
import jax.numpy as jnp
from jax import lax
from jax.experimental import pallas as pl
from jax.experimental.pallas import tpu as pltpu
from jax.sharding import PartitionSpec as P

BLOCK_VOX = 128
KERNEL_TAPS = 3
TAP_SPACING = 8
HRF = 16
MARGIN = (KERNEL_TAPS - 1) * TAP_SPACING
F32 = jnp.float32
BF16 = jnp.bfloat16
NT = (((1,), (1,)), ((), ()))
VMEM = pl.BlockSpec(memory_space=pltpu.VMEM)
SMEM = pl.BlockSpec(memory_space=pltpu.SMEM)
HBM = pl.BlockSpec(memory_space=pltpu.HBM)


def call(body, outs, ins, micros, scratch=()):
    return pl.pallas_call(
        body,
        out_shape=outs,
        in_specs=[spec for spec, _ in ins],
        out_specs=jax.tree.map(lambda _: VMEM, outs),
        scratch_shapes=scratch,
        compiler_params=pltpu.CompilerParams(vmem_limit_bytes=16 << 20),
        cost_estimate=pl.CostEstimate(
            flops=int(micros * 1.15e9), bytes_accessed=int(micros * 1e6), transcendentals=0
        ),
    )(*[value for _, value in ins])


def session_starts(ends, time):
    start = jnp.zeros_like(time)
    for end in ends:
        start = jnp.where(time >= end, end, start)
    return start


def session_stops(ends, time):
    stop = jnp.zeros_like(time)
    for end in reversed(ends):
        stop = jnp.where(time < end, end, stop)
    return stop


def facts_of(ref, blocks):
    row = [ref[at : at + 1, :] for at in range(ref.shape[0])]
    return row[:blocks], row[blocks : 2 * blocks], row[2 * blocks :]


def pack_kernel(
    rows,
    blocks,
    subject_hbm,
    live_hbm,
    lengths_hbm,
    clip_ref,
    bold_ref,
    payload_ref,
    ends_ref,
    facts_ref,
    subject_ref,
    live_ref,
    lengths_ref,
    sems,
):
    slots = bold_ref.shape[1]
    tail = 2 * MARGIN
    moves = [
        (clip_ref.at[pl.ds(rows - tail, tail), :], payload_ref.at[pl.ds(0, tail), :]),
        (clip_ref.at[pl.ds(0, MARGIN), :], payload_ref.at[pl.ds(tail, MARGIN), :]),
        (
            bold_ref.at[pl.ds(0, MARGIN), :],
            payload_ref.at[pl.ds(tail + MARGIN, MARGIN), pl.ds(0, slots)],
        ),
        (subject_hbm, subject_ref),
        (live_hbm, live_ref),
        (lengths_hbm, lengths_ref),
    ]
    copies = [pltpu.make_async_copy(*move, sems.at[at]) for at, move in enumerate(moves)]
    for copy in copies:
        copy.start()
    payload_ref[3 * MARGIN :, slots:] = jnp.zeros_like(payload_ref[3 * MARGIN :, slots:])
    for copy in copies[3:]:
        copy.wait()
    row = lax.broadcasted_iota(jnp.int32, ends_ref.shape, 0)
    last = blocks - 1
    ends = jnp.where(row == 0, subject_ref[0], live_ref[0])
    ends = jnp.where(row == 2, subject_ref[last], ends)
    ends_ref[...] = jnp.where(row == 3, live_ref[last], ends)
    values = [subject_ref[b] for b in range(blocks)] + [live_ref[b] for b in range(blocks)]
    end = jnp.int32(0)
    for at in range(lengths_ref.shape[0]):
        end = end + lengths_ref[at]
        values.append(end)
    row = lax.broadcasted_iota(jnp.int32, facts_ref.shape, 0)
    facts = jnp.full(facts_ref.shape, end, jnp.int32)
    for at, value in enumerate(values):
        facts = jnp.where(row == at, value, facts)
    facts_ref[...] = facts
    for copy in copies[:3]:
        copy.wait()


def conv_kernel(
    rows, blocks, facts_ref, clip_ref, near_ref, far_ref, taps_ref, depth_ref, deep_ref, ext
):
    feats = clip_ref.shape[1]
    odd = lax.axis_index("tm") % 2
    ext[2 * MARGIN : 2 * MARGIN + rows, :] = clip_ref[...]

    @pl.when(odd == 0)
    def _():
        ext[: 2 * MARGIN, :] = far_ref[: 2 * MARGIN, :]
        ext[2 * MARGIN + rows :, :] = near_ref[2 * MARGIN : 3 * MARGIN, :]

    @pl.when(odd == 1)
    def _():
        ext[: 2 * MARGIN, :] = near_ref[: 2 * MARGIN, :]
        ext[2 * MARGIN + rows :, :] = far_ref[2 * MARGIN : 3 * MARGIN, :]

    first = lax.axis_index("tm") * rows - MARGIN
    session_ends = facts_of(facts_ref, blocks)[2]
    taps = [taps_ref[k : k + 1, :] for k in range(KERNEL_TAPS)]
    for at in range(0, rows + 2 * MARGIN, 16):
        time = first + at + lax.broadcasted_iota(jnp.int32, (16, 128), 0)
        since = time - session_starts(session_ends, time)
        values = ext[at : at + 32, :].astype(F32)
        total = taps[0] * values[16:32]
        for k in range(1, KERNEL_TAPS):
            valid = (since >= k * TAP_SPACING).astype(F32)
            shift = MARGIN - k * TAP_SPACING
            moved = values[shift : shift + 16] * jnp.tile(valid, (1, feats // 128))
            total = total + taps[k] * moved
        deep_ref[at : at + 16, :] = total.astype(BF16)
    depth_ref[...] = deep_ref[MARGIN : MARGIN + rows, :]


def core_kernel(
    rows,
    blocks,
    clip_ref,
    near_ref,
    far_ref,
    deep_ref,
    point_ref,
    facts_ref,
    gains_ref,
    weight_ref,
    core_ref,
    effective_ref,
    response_ref,
    ext,
):
    feats = clip_ref.shape[1]
    odd = lax.axis_index("tm") % 2
    ext[MARGIN : MARGIN + rows, :] = clip_ref[...]

    @pl.when(odd == 0)
    def _():
        ext[:MARGIN, :] = far_ref[MARGIN : 2 * MARGIN, :]
        ext[MARGIN + rows :, :] = near_ref[2 * MARGIN : 3 * MARGIN, :]

    @pl.when(odd == 1)
    def _():
        ext[:MARGIN, :] = near_ref[MARGIN : 2 * MARGIN, :]
        ext[MARGIN + rows :, :] = far_ref[2 * MARGIN : 3 * MARGIN, :]

    slots = blocks * BLOCK_VOX
    subjects = gains_ref.shape[0]
    whole = gains_ref[...]
    high = whole.astype(BF16).astype(F32)
    middle = (whole - high).astype(BF16).astype(F32)
    low = whole - high - middle
    terms = jnp.concatenate([high, middle, low], axis=0).astype(BF16)
    owner = jnp.concatenate(facts_of(facts_ref, blocks)[0], axis=1)
    row = lax.broadcasted_iota(jnp.int32, (3 * subjects, slots), 0) % subjects
    pick = jnp.where(row == owner, 1.0, 0.0).astype(BF16)
    scale = lax.dot_general(
        terms, pick, (((0,), (0,)), ((), ())), preferred_element_type=F32
    )
    effective_ref[...] = (weight_ref[...].astype(F32) * scale).astype(BF16)
    for col in range(0, feats, 256):
        lanes = slice(col, col + 256)
        act = jnp.dot(deep_ref[...], point_ref[:, lanes], preferred_element_type=F32)
        core_ref[:, lanes] = (ext[:, lanes].astype(F32) + jax.nn.gelu(act)).astype(BF16)
    for b in range(0, blocks, 2):
        many = min(2, blocks - b)
        lanes = slice(b * BLOCK_VOX, (b + many) * BLOCK_VOX)
        part = jnp.dot(core_ref[...], effective_ref[:, lanes], preferred_element_type=F32)
        part = part.astype(BF16).astype(F32)
        for c in range(many):
            response_ref[b + c] = part[:, c * BLOCK_VOX : (c + 1) * BLOCK_VOX]


def block_at(position, bits):
    return sum(
        ((position >> (len(bits) - 1 - s)) & 1) << bits[s] for s in range(len(bits))
    )


def picked(position, orders):
    even, odd = (block_at(position, bits) for bits in orders)
    mask = jnp.where(lax.axis_index("tm") % 2 == 0, even, odd)
    return lax.axis_index("vox") ^ mask


def spread_taps(hrf_ref, taps):
    for k in range(HRF):
        taps[k] = jnp.broadcast_to(hrf_ref[k : k + 1, :], taps.shape[1:])


def filtered(at, blocks, taps, limit, source, base, step):
    pairs = [(b, h) for b in range(blocks) for h in (0, 8)]
    depth = {h: limit[at + h : at + h + 8, :] for h in (0, 8)}
    total = {}
    for b, h in pairs:
        lanes = slice(b * BLOCK_VOX, (b + 1) * BLOCK_VOX)
        row = at + h + base
        total[b, h] = taps[0, :, lanes] * source[b, row : row + 8, :]
    for k in range(1, HRF):
        valid = {h: depth[h] >= k for h in (0, 8)}
        for b, h in pairs:
            lanes = slice(b * BLOCK_VOX, (b + 1) * BLOCK_VOX)
            row = at + h + base + step * k
            moved = jnp.where(valid[h], source[b, row : row + 8, :], 0.0)
            total[b, h] = total[b, h] + taps[k, :, lanes] * moved
    return total


def forward_kernel(
    rows, blocks, facts_ref, response_ref, hrf_ref, bold_ref, near_ref, far_ref, misfit_ref, bold, since, taps
):
    lead_rows = rows + MARGIN
    slots = blocks * BLOCK_VOX
    odd = lax.axis_index("tm") % 2
    bold[:rows, :] = bold_ref[...]

    @pl.when(odd == 0)
    def _():
        bold[rows:, :] = near_ref[3 * MARGIN :, :slots]

    @pl.when(odd == 1)
    def _():
        bold[rows:, :] = far_ref[3 * MARGIN :, :slots]

    first = lax.axis_index("tm") * rows
    time = first + lax.broadcasted_iota(jnp.int32, (lead_rows, BLOCK_VOX), 0)
    since[...] = time - session_starts(facts_of(facts_ref, blocks)[2], time)
    spread_taps(hrf_ref, taps)
    for at in range(0, lead_rows, 16):
        total = filtered(at, blocks, taps, since, response_ref, MARGIN, -1)
        for b in range(blocks):
            target = bold[at : at + 16, b * BLOCK_VOX : (b + 1) * BLOCK_VOX].astype(F32)
            for h in (0, 8):
                misfit_ref[b, at + h : at + h + 8, :] = total[b, h] - target[h : h + 8]


def backward_kernel(
    rows,
    blocks,
    orders,
    width,
    facts_ref,
    mine_ref,
    twin_ref,
    misfit_ref,
    effective_ref,
    hrf_ref,
    half_ref,
    send_ref,
    loss_ref,
    grads,
    left,
    taps,
):
    lead_rows = rows + MARGIN
    own_subjects, own_lives, session_ends = facts_of(facts_ref, blocks)
    first_core = lax.axis_index("tm") % 2 == 0
    low = jnp.where(first_core, mine_ref[...], twin_ref[...])
    high = jnp.where(first_core, twin_ref[...], mine_ref[...])
    even_vox = lax.axis_index("vox") % 2 == 0
    before = jnp.where(even_vox, high, low)
    after = jnp.where(even_vox, low, high)
    subjects = [before[2:3]] + own_subjects + [after[0:1]]
    lives = [before[3:4]] + own_lives + [after[1:2]]
    lane = lax.broadcasted_iota(jnp.int32, (8, BLOCK_VOX), 1)
    lost = jnp.zeros((8, BLOCK_VOX), F32)
    for b in range(blocks):
        count = lives[b + 1]
        count = count + jnp.where(subjects[b] == subjects[b + 1], lives[b], 0)
        count = count + jnp.where(subjects[b + 2] == subjects[b + 1], lives[b + 2], 0)
        inverse = 1.0 / jnp.maximum(count, 1).astype(F32)
        weight = jnp.where(lane < lives[b + 1], inverse, 0.0)
        double = 2.0 * weight
        for at in range(0, lead_rows, 8):
            misfit = misfit_ref[b, at : at + 8, :]
            grads[b, at : at + 8, :] = double * misfit
            if at < rows:
                lost = lost + weight * misfit * misfit
    loss_ref[...] = lost
    time = lax.axis_index("tm") * rows + lax.broadcasted_iota(jnp.int32, (rows, BLOCK_VOX), 0)
    left[...] = session_stops(session_ends, time) - 1 - time
    spread_taps(hrf_ref, taps)
    for at in range(0, rows, 16):
        total = filtered(at, blocks, taps, left, grads, 0, 1)
        for b in range(blocks):
            half_ref[at : at + 16, b * BLOCK_VOX : (b + 1) * BLOCK_VOX] = jnp.concatenate(
                [total[b, 0], total[b, 8]], axis=0
            ).astype(BF16)
    halves = 1 << (len(orders[0]) - 1)
    send_ref[halves * width :, :] = loss_pair(lost, rows)
    for p in range(halves):
        at = pl.multiple_of(picked(halves + p, orders) * width, width)
        send_ref[p * width : (p + 1) * width, :] = lax.dot_general(
            effective_ref[pl.ds(at, width), :], half_ref[...], NT, preferred_element_type=F32
        ).astype(BF16)


def rest_kernel(
    rows, orders, width, tm_bits, share, core_ref, effective_ref, half_ref, keep_ref, out_ref, own_ref, flipped
):
    halves = 1 << (len(orders[0]) - 1)
    flipped[...] = jnp.transpose(core_ref[MARGIN : MARGIN + rows, :])
    pieces = 1 << len(tm_bits)
    for q in reversed(range(pieces)):
        at = pl.multiple_of((lax.axis_index("tm") ^ block_at(q, tm_bits)) * share, share)
        part = jnp.dot(flipped[pl.ds(at, share), :], half_ref[...], preferred_element_type=F32)
        if q >= pieces // 2:
            slot = q - pieces // 2
            out_ref[slot * share : (slot + 1) * share, :] = part.astype(BF16)
        else:
            own_ref[q * share : (q + 1) * share, :] = part
    for p in range(halves):
        at = pl.multiple_of(picked(p, orders) * width, width)
        keep_ref[p * width : (p + 1) * width, :] = lax.dot_general(
            effective_ref[pl.ds(at, width), :], half_ref[...], NT, preferred_element_type=F32
        )


def slope_kernel(point_ref, depth_ref, slope_ref):
    act = lax.dot_general(
        point_ref[...], depth_ref[...], (((0,), (1,)), ((), ())), preferred_element_type=F32
    )
    slope_ref[...] = jax.vjp(jax.nn.gelu, act)[1](jnp.ones_like(act))[0]


def loss_pair(value, width):
    high = value.astype(BF16).astype(F32)
    pair = jnp.concatenate([high, value - high], axis=0)
    pad = jnp.zeros((16, width - BLOCK_VOX), F32)
    return jnp.concatenate([pair, pad], axis=1).astype(BF16)


def grad_kernel(keep_ref, arrived_ref, lost_ref, slope_ref, out_ref):
    width = keep_ref.shape[0]
    total = keep_ref[...] + arrived_ref[:width, :].astype(F32)
    out_ref[:width, :] = (total * slope_ref[...]).astype(BF16)
    pair = arrived_ref[width:, :BLOCK_VOX].astype(F32)
    out_ref[width:, :] = loss_pair(lost_ref[...] + pair[:8] + pair[8:], keep_ref.shape[1])


def early_kernel(parts, width, *refs):
    grad_refs, depth_refs, (total_ref,) = refs[:parts], refs[parts : 2 * parts], refs[2 * parts :]
    for col in range(0, total_ref.shape[1], 256):
        lanes = slice(col, col + 256)
        total = None
        for grad_ref, depth_ref in zip(grad_refs, depth_refs):
            part = jnp.dot(
                grad_ref[:width, :], depth_ref[:, lanes], preferred_element_type=F32
            )
            total = part if total is None else total + part
        total_ref[:, lanes] = total


def later_kernel(parts, width, before_ref, *refs):
    grad_refs, depth_refs, (total_ref,) = refs[:parts], refs[parts : 2 * parts], refs[2 * parts :]
    for col in range(0, total_ref.shape[1], 256):
        lanes = slice(col, col + 256)
        total = before_ref[:, lanes]
        for grad_ref, depth_ref in zip(grad_refs, depth_refs):
            total = total + jnp.dot(
                grad_ref[:width, :], depth_ref[:, lanes], preferred_element_type=F32
            )
        total_ref[:, lanes] = total


def last_kernel(others, parts, width, scale, total_ref, *refs):
    other_refs = refs[:others]
    grad_refs = refs[others : others + parts]
    depth_refs = refs[others + parts : others + 2 * parts]
    point_ref, loss_ref = refs[others + 2 * parts :]
    lost = None
    for ref in other_refs + grad_refs:
        part = ref[width:, :BLOCK_VOX].astype(F32)
        lost = part if lost is None else lost + part
    loss_ref[0, 0] = jnp.sum(lost) * scale
    for col in range(0, total_ref.shape[1], 256):
        lanes = slice(col, col + 256)
        total = total_ref[:, lanes]
        for grad_ref, depth_ref in zip(grad_refs, depth_refs):
            total = total + jnp.dot(
                grad_ref[:width, :], depth_ref[:, lanes], preferred_element_type=F32
            )
        point_ref[lanes, :] = jnp.transpose(total)


def readout_kernel(blocks, subject_ref, keep_ref, arrived_ref, gains_ref, out_ref):
    rows = [gains_ref[pl.ds(subject_ref[b], 1), :] for b in range(blocks)]
    rows += [rows[-1]] * (-blocks % 8)
    cols = jnp.transpose(jnp.concatenate(rows, axis=0))
    for b in range(blocks):
        lanes = slice(b * BLOCK_VOX, (b + 1) * BLOCK_VOX)
        total = keep_ref[:, lanes] + arrived_ref[:, lanes].astype(F32)
        out_ref[:, lanes] = total * cols[:, b : b + 1]


def shards(
    tm_count,
    vox_count,
    clip_features,
    depth_kernel,
    point_weight,
    session_lengths,
    subject_feature_gains,
    readout_weight,
    hrf_kernel,
    block_subject,
    block_live,
    bold_target,
):
    rows, feats = clip_features.shape
    slots = readout_weight.shape[1]
    blocks = slots // BLOCK_VOX
    subjects = subject_feature_gains.shape[0]
    width = feats // vox_count
    share = feats // tm_count
    vox_bits = list(range(vox_count.bit_length() - 1))
    orders = (vox_bits, [vox_bits[1], vox_bits[0]] + vox_bits[2:])
    tm_bits = list(range(tm_count.bit_length() - 1))

    def swap_tm(value, bit):
        return lax.ppermute(value, "tm", [(i, i ^ (1 << bit)) for i in range(tm_count)])

    def across(value, partner):
        pairs = []
        for t in range(tm_count):
            for v in range(vox_count):
                to = partner(t, v)
                if to is not None:
                    pairs.append((t * vox_count + v, to[0] * vox_count + to[1]))
        return lax.ppermute(value, ("tm", "vox"), pairs)

    def next_tm(t, v):
        other = t + 1 if t % 2 else t - 1
        return (other, v) if 0 <= other < tm_count else None

    def next_vox(t, v):
        if t % 2 == 0:
            return (t, v ^ 1)
        other = v + 1 if v % 2 else v - 1
        return (t, other) if 0 <= other < vox_count else None

    fact_rows = 2 * blocks + session_lengths.shape[0]
    fact_rows += -fact_rows % 8
    payload, ends, facts = pl.pallas_call(
        functools.partial(pack_kernel, rows, blocks),
        out_shape=(
            pltpu.VMEM((4 * MARGIN, feats), BF16),
            pltpu.VMEM((8, BLOCK_VOX), jnp.int32),
            pltpu.VMEM((fact_rows, BLOCK_VOX), jnp.int32),
        ),
        in_specs=[HBM] * 5,
        out_specs=(VMEM, VMEM, VMEM),
        scratch_shapes=[
            pltpu.SMEM((blocks,), jnp.int32),
            pltpu.SMEM((blocks,), jnp.int32),
            pltpu.SMEM(session_lengths.shape, jnp.int32),
            pltpu.SemaphoreType.DMA((6,)),
        ],
        cost_estimate=pl.CostEstimate(
            flops=int(6 * 1.15e9), bytes_accessed=1000000, transcendentals=0
        ),
    )(
        *[
            pltpu.with_memory_space_constraint(value, pltpu.HBM)
            for value in (block_subject, block_live, session_lengths, clip_features, bold_target)
        ]
    )
    far = across(payload, next_tm)
    mine = across(ends, next_vox)
    near = swap_tm(payload, 0)

    halos = [(VMEM, clip_features), (VMEM, near), (VMEM, far)]
    depth_half, deep = call(
        functools.partial(conv_kernel, rows, blocks),
        (
            jax.ShapeDtypeStruct((rows, feats), BF16),
            jax.ShapeDtypeStruct((rows + 2 * MARGIN, feats), BF16),
        ),
        [(VMEM, facts)] + halos + [(VMEM, depth_kernel)],
        0.1,
        [pltpu.VMEM((rows + 3 * MARGIN, feats), BF16)],
    )
    core_out, effective, response = call(
        functools.partial(core_kernel, rows, blocks),
        (
            jax.ShapeDtypeStruct((rows + 2 * MARGIN, feats), BF16),
            jax.ShapeDtypeStruct((feats, slots), BF16),
            jax.ShapeDtypeStruct((blocks, rows + 2 * MARGIN, BLOCK_VOX), F32),
        ),
        halos
        + [(VMEM, deep), (VMEM, point_weight), (VMEM, facts)]
        + [(VMEM, subject_feature_gains), (VMEM, readout_weight)],
        1.0,
        [pltpu.VMEM((rows + 2 * MARGIN, feats), BF16)],
    )
    response, mine = lax.optimization_barrier((response, mine))
    twin = swap_tm(mine, 0)
    misfit = call(
        functools.partial(forward_kernel, rows, blocks),
        jax.ShapeDtypeStruct((blocks, rows + MARGIN, BLOCK_VOX), F32),
        [
            (VMEM, facts),
            (VMEM, response),
            (VMEM, hrf_kernel),
            (VMEM, bold_target),
            (VMEM, near),
            (VMEM, far),
        ],
        1.5,
        [
            pltpu.VMEM((rows + MARGIN, slots), BF16),
            pltpu.VMEM((rows + MARGIN, BLOCK_VOX), jnp.int32),
            pltpu.VMEM((HRF, 8, slots), F32),
        ],
    )
    half, send, lost = call(
        functools.partial(backward_kernel, rows, blocks, orders, width),
        (
            jax.ShapeDtypeStruct((rows, slots), BF16),
            jax.ShapeDtypeStruct((feats // 2 + 16, rows), BF16),
            jax.ShapeDtypeStruct((8, BLOCK_VOX), F32),
        ),
        [
            (VMEM, facts),
            (VMEM, mine),
            (VMEM, twin),
            (VMEM, misfit),
            (VMEM, effective),
            (VMEM, hrf_kernel),
        ],
        2.5,
        [
            pltpu.VMEM((blocks, rows + MARGIN, BLOCK_VOX), F32),
            pltpu.VMEM((rows, BLOCK_VOX), jnp.int32),
            pltpu.VMEM((HRF, 8, slots), F32),
        ],
    )
    keep, raw_send, raw_keep = call(
        functools.partial(rest_kernel, rows, orders, width, tm_bits, share),
        (
            jax.ShapeDtypeStruct((feats // 2, rows), F32),
            jax.ShapeDtypeStruct((feats // 2, slots), BF16),
            jax.ShapeDtypeStruct((feats // 2, slots), F32),
        ),
        [(VMEM, core_out), (VMEM, effective), (VMEM, half)],
        1.1,
        [pltpu.VMEM((feats, rows), BF16)],
    )

    def loss_rows(value):
        high = lax.reduce_precision(value, 8, 7)
        pair = jnp.concatenate([high, value - high], axis=0)
        return jnp.pad(pair, ((0, 0), (0, rows - BLOCK_VOX))).astype(BF16)

    def loss_of(arrived):
        pair = arrived[:, :BLOCK_VOX].astype(F32)
        return pair[:8] + pair[8:]

    col = lax.axis_index("vox") * width
    point_cols = lax.dynamic_slice_in_dim(point_weight, col, width, 1)
    slope = call(
        slope_kernel,
        jax.ShapeDtypeStruct((width, rows), F32),
        [(VMEM, point_cols), (VMEM, depth_half)],
        0.7,
    )
    own_gains = lax.dynamic_slice_in_dim(
        subject_feature_gains, lax.axis_index("tm") * share, share, 1
    )
    stages = len(vox_bits)
    paths = [()]
    for bit in reversed(tm_bits):
        paths = paths + [path + (bit,) for path in paths]
    depths = {(): depth_half}
    first = [(bit,) for bit in reversed(tm_bits)]
    for path in first:
        depths[path] = swap_tm(depth_half, path[0])
    raw_came = swap_tm(raw_send, tm_bits[0])
    for stage in range(stages):
        arrived = across(send, lambda t, v: (t, v ^ (1 << orders[t % 2][stage])))
        if stage == 0:
            held = lax.optimization_barrier((arrived, *[depths[path] for path in first]))
            arrived = held[0]
            depths.update(zip(first, held[1:]))
        if stage == min(1, stages - 1):
            for bit in tm_bits[1:]:
                raw_keep = raw_keep + raw_came.astype(F32)
                size = raw_keep.shape[0] // 2
                raw_send, raw_keep = raw_keep[size:].astype(BF16), raw_keep[:size]
                raw_came = swap_tm(raw_send, bit)
            arrived, raw_keep, slope, own_gains = lax.optimization_barrier(
                (arrived, raw_keep, slope, own_gains)
            )
        if stage + 1 < stages:
            size = keep.shape[0] // 2
            keep = keep + arrived[: 2 * size].astype(F32)
            lost = lost + loss_of(arrived[2 * size :])
            send = jnp.concatenate([keep[size:].astype(BF16), loss_rows(lost)], axis=0)
            keep = keep[:size]
    arrived, raw_came = lax.optimization_barrier((arrived, raw_came))
    for path in paths[1:]:
        if path not in depths:
            depths[path] = swap_tm(depths[path[:-1]], path[-1])
    pre_grad = call(
        grad_kernel,
        jax.ShapeDtypeStruct((width + 16, rows), BF16),
        [(VMEM, keep), (VMEM, arrived), (VMEM, lost), (VMEM, slope)],
        0.3,
    )
    groups = [[(), (0,)], [path for path in paths[1:] if path[-1] != 0]]
    groups.append([path for path in paths if path not in groups[0] + groups[1]])

    def operands(group):
        return [(VMEM, grads[path]) for path in group] + [(VMEM, depths[path]) for path in group]

    grads = {(): pre_grad}
    for path in groups[0][1:] + groups[1]:
        grads[path] = swap_tm(grads[path[:-1]], path[-1])
    total_shape = jax.ShapeDtypeStruct((width, feats), F32)
    total = call(
        functools.partial(early_kernel, len(groups[0]), width), total_shape, operands(groups[0]), 0.3
    )
    top = groups[1][-1]
    grad_readout = call(
        functools.partial(readout_kernel, blocks),
        jax.ShapeDtypeStruct((share, slots), F32),
        [(SMEM, block_subject), (VMEM, raw_keep), (VMEM, raw_came), (VMEM, own_gains)],
        0.8,
    )
    grads[top], total, grad_readout = lax.optimization_barrier(
        (grads[top], total, grad_readout)
    )
    for path in groups[2]:
        grads[path] = swap_tm(grads[path[:-1]], path[-1])
    total = call(
        functools.partial(later_kernel, len(groups[1]), width),
        total_shape,
        [(VMEM, total)] + operands(groups[1]),
        0.3,
    )
    others = groups[0] + groups[1]
    ins = [(VMEM, total)] + [(VMEM, grads[path]) for path in others] + operands(groups[2])
    grad_point, loss_total = pl.pallas_call(
        functools.partial(
            last_kernel, len(others), len(groups[2]), width, 1.0 / (subjects * rows * tm_count)
        ),
        out_shape=(
            jax.ShapeDtypeStruct((feats, width), F32),
            jax.ShapeDtypeStruct((1, 1), F32),
        ),
        in_specs=[spec for spec, _ in ins],
        out_specs=(VMEM, SMEM),
        compiler_params=pltpu.CompilerParams(vmem_limit_bytes=16 << 20),
        cost_estimate=pl.CostEstimate(
            flops=int(1.15e9), bytes_accessed=1000000, transcendentals=0
        ),
    )(*[value for _, value in ins])
    return (loss_total.reshape(()), grad_readout, grad_point)


def solution(mesh):
    placed = (
        P("tm", None),
        P(),
        P(),
        P(),
        P(),
        P(None, "vox"),
        P(None, "vox"),
        P("vox"),
        P("vox"),
        P("tm", "vox"),
    )
    return jax.shard_map(
        functools.partial(shards, mesh.shape["tm"], mesh.shape["vox"]),
        mesh=mesh,
        in_specs=placed,
        out_specs=(P(), P("tm", "vox"), P(None, "vox")),
        check_vma=False,
    )
```

```python
import functools
import jax
import jax.numpy as jnp
from jax import lax
from jax.experimental import pallas as pl
from jax.experimental.pallas import tpu as pltpu
from jax.sharding import PartitionSpec as P

BLOCK_VOX = 128
KERNEL_TAPS = 3
TAP_SPACING = 8
HRF = 16
MARGIN = (KERNEL_TAPS - 1) * TAP_SPACING
F32 = jnp.float32
BF16 = jnp.bfloat16
NT = (((1,), (1,)), ((), ()))
VMEM = pl.BlockSpec(memory_space=pltpu.VMEM)
SMEM = pl.BlockSpec(memory_space=pltpu.SMEM)
HBM = pl.BlockSpec(memory_space=pltpu.HBM)


def call(body, outs, ins, micros, scratch=()):
    return pl.pallas_call(
        body,
        out_shape=outs,
        in_specs=[spec for spec, _ in ins],
        out_specs=jax.tree.map(lambda _: VMEM, outs),
        scratch_shapes=scratch,
        compiler_params=pltpu.CompilerParams(vmem_limit_bytes=16 << 20),
        cost_estimate=pl.CostEstimate(
            flops=int(micros * 1.15e9), bytes_accessed=int(micros * 1e6), transcendentals=0
        ),
    )(*[value for _, value in ins])


def session_starts(ends, time):
    start = jnp.zeros_like(time)
    for end in ends:
        start = jnp.where(time >= end, end, start)
    return start


def session_stops(ends, time):
    stop = jnp.zeros_like(time)
    for end in reversed(ends):
        stop = jnp.where(time < end, end, stop)
    return stop


def facts_of(ref, blocks):
    row = [ref[at : at + 1, :] for at in range(ref.shape[0])]
    return row[:blocks], row[blocks : 2 * blocks], row[2 * blocks :]


def pack_kernel(
    rows,
    blocks,
    subject_hbm,
    live_hbm,
    lengths_hbm,
    clip_ref,
    bold_ref,
    payload_ref,
    ends_ref,
    facts_ref,
    subject_ref,
    live_ref,
    lengths_ref,
    sems,
):
    slots = bold_ref.shape[1]
    tail = 2 * MARGIN
    moves = [
        (clip_ref.at[pl.ds(rows - tail, tail), :], payload_ref.at[pl.ds(0, tail), :]),
        (clip_ref.at[pl.ds(0, MARGIN), :], payload_ref.at[pl.ds(tail, MARGIN), :]),
        (
            bold_ref.at[pl.ds(0, MARGIN), :],
            payload_ref.at[pl.ds(tail + MARGIN, MARGIN), pl.ds(0, slots)],
        ),
        (subject_hbm, subject_ref),
        (live_hbm, live_ref),
        (lengths_hbm, lengths_ref),
    ]
    copies = [pltpu.make_async_copy(*move, sems.at[at]) for at, move in enumerate(moves)]
    for copy in copies:
        copy.start()
    payload_ref[3 * MARGIN :, slots:] = jnp.zeros_like(payload_ref[3 * MARGIN :, slots:])
    for copy in copies[3:]:
        copy.wait()
    row = lax.broadcasted_iota(jnp.int32, ends_ref.shape, 0)
    last = blocks - 1
    ends = jnp.where(row == 0, subject_ref[0], live_ref[0])
    ends = jnp.where(row == 2, subject_ref[last], ends)
    ends_ref[...] = jnp.where(row == 3, live_ref[last], ends)
    values = [subject_ref[b] for b in range(blocks)] + [live_ref[b] for b in range(blocks)]
    end = jnp.int32(0)
    for at in range(lengths_ref.shape[0]):
        end = end + lengths_ref[at]
        values.append(end)
    row = lax.broadcasted_iota(jnp.int32, facts_ref.shape, 0)
    facts = jnp.full(facts_ref.shape, end, jnp.int32)
    for at, value in enumerate(values):
        facts = jnp.where(row == at, value, facts)
    facts_ref[...] = facts
    for copy in copies[:3]:
        copy.wait()


def conv_kernel(
    rows, blocks, facts_ref, clip_ref, near_ref, far_ref, taps_ref, depth_ref, deep_ref, ext
):
    feats = clip_ref.shape[1]
    odd = lax.axis_index("tm") % 2
    ext[2 * MARGIN : 2 * MARGIN + rows, :] = clip_ref[...]

    @pl.when(odd == 0)
    def _():
        ext[: 2 * MARGIN, :] = far_ref[: 2 * MARGIN, :]
        ext[2 * MARGIN + rows :, :] = near_ref[2 * MARGIN : 3 * MARGIN, :]

    @pl.when(odd == 1)
    def _():
        ext[: 2 * MARGIN, :] = near_ref[: 2 * MARGIN, :]
        ext[2 * MARGIN + rows :, :] = far_ref[2 * MARGIN : 3 * MARGIN, :]

    first = lax.axis_index("tm") * rows - MARGIN
    session_ends = facts_of(facts_ref, blocks)[2]
    taps = [taps_ref[k : k + 1, :] for k in range(KERNEL_TAPS)]
    for at in range(0, rows + 2 * MARGIN, 16):
        time = first + at + lax.broadcasted_iota(jnp.int32, (16, 128), 0)
        since = time - session_starts(session_ends, time)
        values = ext[at : at + 32, :].astype(F32)
        total = taps[0] * values[16:32]
        for k in range(1, KERNEL_TAPS):
            valid = (since >= k * TAP_SPACING).astype(F32)
            shift = MARGIN - k * TAP_SPACING
            moved = values[shift : shift + 16] * jnp.tile(valid, (1, feats // 128))
            total = total + taps[k] * moved
        deep_ref[at : at + 16, :] = total.astype(BF16)
    depth_ref[...] = deep_ref[MARGIN : MARGIN + rows, :]


def core_kernel(
    rows,
    blocks,
    clip_ref,
    near_ref,
    far_ref,
    deep_ref,
    point_ref,
    facts_ref,
    gains_ref,
    weight_ref,
    core_ref,
    effective_ref,
    response_ref,
    ext,
):
    feats = clip_ref.shape[1]
    odd = lax.axis_index("tm") % 2
    ext[MARGIN : MARGIN + rows, :] = clip_ref[...]

    @pl.when(odd == 0)
    def _():
        ext[:MARGIN, :] = far_ref[MARGIN : 2 * MARGIN, :]
        ext[MARGIN + rows :, :] = near_ref[2 * MARGIN : 3 * MARGIN, :]

    @pl.when(odd == 1)
    def _():
        ext[:MARGIN, :] = near_ref[MARGIN : 2 * MARGIN, :]
        ext[MARGIN + rows :, :] = far_ref[2 * MARGIN : 3 * MARGIN, :]

    slots = blocks * BLOCK_VOX
    subjects = gains_ref.shape[0]
    whole = gains_ref[...]
    high = whole.astype(BF16).astype(F32)
    middle = (whole - high).astype(BF16).astype(F32)
    low = whole - high - middle
    terms = jnp.concatenate([high, middle, low], axis=0).astype(BF16)
    owner = jnp.concatenate(facts_of(facts_ref, blocks)[0], axis=1)
    row = lax.broadcasted_iota(jnp.int32, (3 * subjects, slots), 0) % subjects
    pick = jnp.where(row == owner, 1.0, 0.0).astype(BF16)
    scale = lax.dot_general(
        terms, pick, (((0,), (0,)), ((), ())), preferred_element_type=F32
    )
    effective_ref[...] = (weight_ref[...].astype(F32) * scale).astype(BF16)
    for col in range(0, feats, 256):
        lanes = slice(col, col + 256)
        act = jnp.dot(deep_ref[...], point_ref[:, lanes], preferred_element_type=F32)
        core_ref[:, lanes] = (ext[:, lanes].astype(F32) + jax.nn.gelu(act)).astype(BF16)
    for b in range(0, blocks, 2):
        many = min(2, blocks - b)
        lanes = slice(b * BLOCK_VOX, (b + many) * BLOCK_VOX)
        part = jnp.dot(core_ref[...], effective_ref[:, lanes], preferred_element_type=F32)
        part = part.astype(BF16).astype(F32)
        for c in range(many):
            response_ref[b + c] = part[:, c * BLOCK_VOX : (c + 1) * BLOCK_VOX]


def block_at(position, bits):
    return sum(
        ((position >> (len(bits) - 1 - s)) & 1) << bits[s] for s in range(len(bits))
    )


def picked(position, orders):
    even, odd = (block_at(position, bits) for bits in orders)
    mask = jnp.where(lax.axis_index("tm") % 2 == 0, even, odd)
    return lax.axis_index("vox") ^ mask


def spread_taps(hrf_ref, taps):
    for k in range(HRF):
        taps[k] = jnp.broadcast_to(hrf_ref[k : k + 1, :], taps.shape[1:])


def filtered(at, blocks, taps, limit, source, base, step):
    pairs = [(b, h) for b in range(blocks) for h in (0, 8)]
    depth = {h: limit[at + h : at + h + 8, :] for h in (0, 8)}
    total = {}
    for b, h in pairs:
        lanes = slice(b * BLOCK_VOX, (b + 1) * BLOCK_VOX)
        row = at + h + base
        total[b, h] = taps[0, :, lanes] * source[b, row : row + 8, :]
    for k in range(1, HRF):
        valid = {h: depth[h] >= k for h in (0, 8)}
        for b, h in pairs:
            lanes = slice(b * BLOCK_VOX, (b + 1) * BLOCK_VOX)
            row = at + h + base + step * k
            moved = jnp.where(valid[h], source[b, row : row + 8, :], 0.0)
            total[b, h] = total[b, h] + taps[k, :, lanes] * moved
    return total


def forward_kernel(
    rows, blocks, facts_ref, response_ref, hrf_ref, bold_ref, near_ref, far_ref, misfit_ref, bold, since, taps
):
    lead_rows = rows + MARGIN
    slots = blocks * BLOCK_VOX
    odd = lax.axis_index("tm") % 2
    bold[:rows, :] = bold_ref[...]

    @pl.when(odd == 0)
    def _():
        bold[rows:, :] = near_ref[3 * MARGIN :, :slots]

    @pl.when(odd == 1)
    def _():
        bold[rows:, :] = far_ref[3 * MARGIN :, :slots]

    first = lax.axis_index("tm") * rows
    time = first + lax.broadcasted_iota(jnp.int32, (lead_rows, BLOCK_VOX), 0)
    since[...] = time - session_starts(facts_of(facts_ref, blocks)[2], time)
    spread_taps(hrf_ref, taps)
    for at in range(0, lead_rows, 16):
        total = filtered(at, blocks, taps, since, response_ref, MARGIN, -1)
        for b in range(blocks):
            target = bold[at : at + 16, b * BLOCK_VOX : (b + 1) * BLOCK_VOX].astype(F32)
            for h in (0, 8):
                misfit_ref[b, at + h : at + h + 8, :] = total[b, h] - target[h : h + 8]


def backward_kernel(
    rows,
    blocks,
    orders,
    width,
    facts_ref,
    mine_ref,
    twin_ref,
    misfit_ref,
    effective_ref,
    hrf_ref,
    half_ref,
    send_ref,
    loss_ref,
    grads,
    left,
    taps,
):
    lead_rows = rows + MARGIN
    own_subjects, own_lives, session_ends = facts_of(facts_ref, blocks)
    first_core = lax.axis_index("tm") % 2 == 0
    low = jnp.where(first_core, mine_ref[...], twin_ref[...])
    high = jnp.where(first_core, twin_ref[...], mine_ref[...])
    even_vox = lax.axis_index("vox") % 2 == 0
    before = jnp.where(even_vox, high, low)
    after = jnp.where(even_vox, low, high)
    subjects = [before[2:3]] + own_subjects + [after[0:1]]
    lives = [before[3:4]] + own_lives + [after[1:2]]
    lane = lax.broadcasted_iota(jnp.int32, (8, BLOCK_VOX), 1)
    lost = jnp.zeros((8, BLOCK_VOX), F32)
    for b in range(blocks):
        count = lives[b + 1]
        count = count + jnp.where(subjects[b] == subjects[b + 1], lives[b], 0)
        count = count + jnp.where(subjects[b + 2] == subjects[b + 1], lives[b + 2], 0)
        inverse = 1.0 / jnp.maximum(count, 1).astype(F32)
        weight = jnp.where(lane < lives[b + 1], inverse, 0.0)
        double = 2.0 * weight
        for at in range(0, lead_rows, 8):
            misfit = misfit_ref[b, at : at + 8, :]
            grads[b, at : at + 8, :] = double * misfit
            if at < rows:
                lost = lost + weight * misfit * misfit
    loss_ref[...] = lost
    time = lax.axis_index("tm") * rows + lax.broadcasted_iota(jnp.int32, (rows, BLOCK_VOX), 0)
    left[...] = session_stops(session_ends, time) - 1 - time
    spread_taps(hrf_ref, taps)
    for at in range(0, rows, 16):
        total = filtered(at, blocks, taps, left, grads, 0, 1)
        for b in range(blocks):
            half_ref[at : at + 16, b * BLOCK_VOX : (b + 1) * BLOCK_VOX] = jnp.concatenate(
                [total[b, 0], total[b, 8]], axis=0
            ).astype(BF16)
    halves = 1 << (len(orders[0]) - 1)
    send_ref[halves * width :, :] = loss_pair(lost, rows)
    for p in range(halves):
        at = pl.multiple_of(picked(halves + p, orders) * width, width)
        send_ref[p * width : (p + 1) * width, :] = lax.dot_general(
            effective_ref[pl.ds(at, width), :], half_ref[...], NT, preferred_element_type=F32
        ).astype(BF16)


def rest_kernel(
    rows, orders, width, tm_bits, share, core_ref, effective_ref, half_ref, keep_ref, out_ref, own_ref, flipped
):
    halves = 1 << (len(orders[0]) - 1)
    flipped[...] = jnp.transpose(core_ref[MARGIN : MARGIN + rows, :])
    pieces = 1 << len(tm_bits)
    for q in reversed(range(pieces)):
        at = pl.multiple_of((lax.axis_index("tm") ^ block_at(q, tm_bits)) * share, share)
        part = jnp.dot(flipped[pl.ds(at, share), :], half_ref[...], preferred_element_type=F32)
        if q >= pieces // 2:
            slot = q - pieces // 2
            out_ref[slot * share : (slot + 1) * share, :] = part.astype(BF16)
        else:
            own_ref[q * share : (q + 1) * share, :] = part
    for p in range(halves):
        at = pl.multiple_of(picked(p, orders) * width, width)
        keep_ref[p * width : (p + 1) * width, :] = lax.dot_general(
            effective_ref[pl.ds(at, width), :], half_ref[...], NT, preferred_element_type=F32
        )


def slope_kernel(point_ref, depth_ref, slope_ref):
    act = lax.dot_general(
        point_ref[...], depth_ref[...], (((0,), (1,)), ((), ())), preferred_element_type=F32
    )
    slope_ref[...] = jax.vjp(jax.nn.gelu, act)[1](jnp.ones_like(act))[0]


def loss_pair(value, width):
    high = value.astype(BF16).astype(F32)
    pair = jnp.concatenate([high, value - high], axis=0)
    pad = jnp.zeros((16, width - BLOCK_VOX), F32)
    return jnp.concatenate([pair, pad], axis=1).astype(BF16)


def grad_kernel(keep_ref, arrived_ref, lost_ref, slope_ref, out_ref):
    width = keep_ref.shape[0]
    total = keep_ref[...] + arrived_ref[:width, :].astype(F32)
    out_ref[:width, :] = (total * slope_ref[...]).astype(BF16)
    pair = arrived_ref[width:, :BLOCK_VOX].astype(F32)
    out_ref[width:, :] = loss_pair(lost_ref[...] + pair[:8] + pair[8:], keep_ref.shape[1])


def early_kernel(parts, width, *refs):
    grad_refs, depth_refs, (total_ref,) = refs[:parts], refs[parts : 2 * parts], refs[2 * parts :]
    for col in range(0, total_ref.shape[1], 256):
        lanes = slice(col, col + 256)
        total = None
        for grad_ref, depth_ref in zip(grad_refs, depth_refs):
            part = jnp.dot(
                grad_ref[:width, :], depth_ref[:, lanes], preferred_element_type=F32
            )
            total = part if total is None else total + part
        total_ref[:, lanes] = total


def later_kernel(parts, width, before_ref, *refs):
    grad_refs, depth_refs, (total_ref,) = refs[:parts], refs[parts : 2 * parts], refs[2 * parts :]
    for col in range(0, total_ref.shape[1], 256):
        lanes = slice(col, col + 256)
        total = before_ref[:, lanes]
        for grad_ref, depth_ref in zip(grad_refs, depth_refs):
            total = total + jnp.dot(
                grad_ref[:width, :], depth_ref[:, lanes], preferred_element_type=F32
            )
        total_ref[:, lanes] = total


def last_kernel(others, parts, width, scale, total_ref, *refs):
    other_refs = refs[:others]
    grad_refs = refs[others : others + parts]
    depth_refs = refs[others + parts : others + 2 * parts]
    point_ref, loss_ref = refs[others + 2 * parts :]
    lost = None
    for ref in other_refs + grad_refs:
        part = ref[width:, :BLOCK_VOX].astype(F32)
        lost = part if lost is None else lost + part
    loss_ref[0, 0] = jnp.sum(lost) * scale
    for col in range(0, total_ref.shape[1], 256):
        lanes = slice(col, col + 256)
        total = total_ref[:, lanes]
        for grad_ref, depth_ref in zip(grad_refs, depth_refs):
            total = total + jnp.dot(
                grad_ref[:width, :], depth_ref[:, lanes], preferred_element_type=F32
            )
        point_ref[lanes, :] = jnp.transpose(total)


def readout_kernel(blocks, subject_ref, keep_ref, arrived_ref, gains_ref, out_ref):
    rows = [gains_ref[pl.ds(subject_ref[b], 1), :] for b in range(blocks)]
    rows += [rows[-1]] * (-blocks % 8)
    cols = jnp.transpose(jnp.concatenate(rows, axis=0))
    for b in range(blocks):
        lanes = slice(b * BLOCK_VOX, (b + 1) * BLOCK_VOX)
        total = keep_ref[:, lanes] + arrived_ref[:, lanes].astype(F32)
        out_ref[:, lanes] = total * cols[:, b : b + 1]


def shards(
    tm_count,
    vox_count,
    clip_features,
    depth_kernel,
    point_weight,
    session_lengths,
    subject_feature_gains,
    readout_weight,
    hrf_kernel,
    block_subject,
    block_live,
    bold_target,
):
    rows, feats = clip_features.shape
    slots = readout_weight.shape[1]
    blocks = slots // BLOCK_VOX
    subjects = subject_feature_gains.shape[0]
    width = feats // vox_count
    share = feats // tm_count
    vox_bits = list(range(vox_count.bit_length() - 1))
    orders = (vox_bits, [vox_bits[1], vox_bits[0]] + vox_bits[2:])
    tm_bits = list(range(tm_count.bit_length() - 1))

    def swap_tm(value, bit):
        return lax.ppermute(value, "tm", [(i, i ^ (1 << bit)) for i in range(tm_count)])

    def across(value, partner):
        pairs = []
        for t in range(tm_count):
            for v in range(vox_count):
                to = partner(t, v)
                if to is not None:
                    pairs.append((t * vox_count + v, to[0] * vox_count + to[1]))
        return lax.ppermute(value, ("tm", "vox"), pairs)

    def next_tm(t, v):
        other = t + 1 if t % 2 else t - 1
        return (other, v) if 0 <= other < tm_count else None

    def next_vox(t, v):
        if t % 2 == 0:
            return (t, v ^ 1)
        other = v + 1 if v % 2 else v - 1
        return (t, other) if 0 <= other < vox_count else None

    fact_rows = 2 * blocks + session_lengths.shape[0]
    fact_rows += -fact_rows % 8
    payload, ends, facts = pl.pallas_call(
        functools.partial(pack_kernel, rows, blocks),
        out_shape=(
            pltpu.VMEM((4 * MARGIN, feats), BF16),
            pltpu.VMEM((8, BLOCK_VOX), jnp.int32),
            pltpu.VMEM((fact_rows, BLOCK_VOX), jnp.int32),
        ),
        in_specs=[HBM] * 5,
        out_specs=(VMEM, VMEM, VMEM),
        scratch_shapes=[
            pltpu.SMEM((blocks,), jnp.int32),
            pltpu.SMEM((blocks,), jnp.int32),
            pltpu.SMEM(session_lengths.shape, jnp.int32),
            pltpu.SemaphoreType.DMA((6,)),
        ],
        cost_estimate=pl.CostEstimate(
            flops=int(6 * 1.15e9), bytes_accessed=1000000, transcendentals=0
        ),
    )(
        *[
            pltpu.with_memory_space_constraint(value, pltpu.HBM)
            for value in (block_subject, block_live, session_lengths, clip_features, bold_target)
        ]
    )
    far = across(payload, next_tm)
    mine = across(ends, next_vox)
    near = swap_tm(payload, 0)

    halos = [(VMEM, clip_features), (VMEM, near), (VMEM, far)]
    depth_half, deep = call(
        functools.partial(conv_kernel, rows, blocks),
        (
            jax.ShapeDtypeStruct((rows, feats), BF16),
            jax.ShapeDtypeStruct((rows + 2 * MARGIN, feats), BF16),
        ),
        [(VMEM, facts)] + halos + [(VMEM, depth_kernel)],
        0.1,
        [pltpu.VMEM((rows + 3 * MARGIN, feats), BF16)],
    )
    core_out, effective, response = call(
        functools.partial(core_kernel, rows, blocks),
        (
            jax.ShapeDtypeStruct((rows + 2 * MARGIN, feats), BF16),
            jax.ShapeDtypeStruct((feats, slots), BF16),
            jax.ShapeDtypeStruct((blocks, rows + 2 * MARGIN, BLOCK_VOX), F32),
        ),
        halos
        + [(VMEM, deep), (VMEM, point_weight), (VMEM, facts)]
        + [(VMEM, subject_feature_gains), (VMEM, readout_weight)],
        1.0,
        [pltpu.VMEM((rows + 2 * MARGIN, feats), BF16)],
    )
    response, mine = lax.optimization_barrier((response, mine))
    twin = swap_tm(mine, 0)
    misfit = call(
        functools.partial(forward_kernel, rows, blocks),
        jax.ShapeDtypeStruct((blocks, rows + MARGIN, BLOCK_VOX), F32),
        [
            (VMEM, facts),
            (VMEM, response),
            (VMEM, hrf_kernel),
            (VMEM, bold_target),
            (VMEM, near),
            (VMEM, far),
        ],
        1.5,
        [
            pltpu.VMEM((rows + MARGIN, slots), BF16),
            pltpu.VMEM((rows + MARGIN, BLOCK_VOX), jnp.int32),
            pltpu.VMEM((HRF, 8, slots), F32),
        ],
    )
    half, send, lost = call(
        functools.partial(backward_kernel, rows, blocks, orders, width),
        (
            jax.ShapeDtypeStruct((rows, slots), BF16),
            jax.ShapeDtypeStruct((feats // 2 + 16, rows), BF16),
            jax.ShapeDtypeStruct((8, BLOCK_VOX), F32),
        ),
        [
            (VMEM, facts),
            (VMEM, mine),
            (VMEM, twin),
            (VMEM, misfit),
            (VMEM, effective),
            (VMEM, hrf_kernel),
        ],
        2.5,
        [
            pltpu.VMEM((blocks, rows + MARGIN, BLOCK_VOX), F32),
            pltpu.VMEM((rows, BLOCK_VOX), jnp.int32),
            pltpu.VMEM((HRF, 8, slots), F32),
        ],
    )
    keep, raw_send, raw_keep = call(
        functools.partial(rest_kernel, rows, orders, width, tm_bits, share),
        (
            jax.ShapeDtypeStruct((feats // 2, rows), F32),
            jax.ShapeDtypeStruct((feats // 2, slots), BF16),
            jax.ShapeDtypeStruct((feats // 2, slots), F32),
        ),
        [(VMEM, core_out), (VMEM, effective), (VMEM, half)],
        1.1,
        [pltpu.VMEM((feats, rows), BF16)],
    )

    def loss_rows(value):
        high = lax.reduce_precision(value, 8, 7)
        pair = jnp.concatenate([high, value - high], axis=0)
        return jnp.pad(pair, ((0, 0), (0, rows - BLOCK_VOX))).astype(BF16)

    def loss_of(arrived):
        pair = arrived[:, :BLOCK_VOX].astype(F32)
        return pair[:8] + pair[8:]

    col = lax.axis_index("vox") * width
    point_cols = lax.dynamic_slice_in_dim(point_weight, col, width, 1)
    slope = call(
        slope_kernel,
        jax.ShapeDtypeStruct((width, rows), F32),
        [(VMEM, point_cols), (VMEM, depth_half)],
        0.7,
    )
    own_gains = lax.dynamic_slice_in_dim(
        subject_feature_gains, lax.axis_index("tm") * share, share, 1
    )
    stages = len(vox_bits)
    paths = [()]
    for bit in reversed(tm_bits):
        paths = paths + [path + (bit,) for path in paths]
    depths = {(): depth_half}
    first = [(bit,) for bit in reversed(tm_bits)]
    for path in first:
        depths[path] = swap_tm(depth_half, path[0])
    raw_came = swap_tm(raw_send, tm_bits[0])
    for stage in range(stages):
        arrived = across(send, lambda t, v: (t, v ^ (1 << orders[t % 2][stage])))
        if stage == 0:
            held = lax.optimization_barrier((arrived, *[depths[path] for path in first]))
            arrived = held[0]
            depths.update(zip(first, held[1:]))
        if stage == min(1, stages - 1):
            for bit in tm_bits[1:]:
                raw_keep = raw_keep + raw_came.astype(F32)
                size = raw_keep.shape[0] // 2
                raw_send, raw_keep = raw_keep[size:].astype(BF16), raw_keep[:size]
                raw_came = swap_tm(raw_send, bit)
            arrived, raw_keep, slope, own_gains = lax.optimization_barrier(
                (arrived, raw_keep, slope, own_gains)
            )
        if stage + 1 < stages:
            size = keep.shape[0] // 2
            keep = keep + arrived[: 2 * size].astype(F32)
            lost = lost + loss_of(arrived[2 * size :])
            send = jnp.concatenate([keep[size:].astype(BF16), loss_rows(lost)], axis=0)
            keep = keep[:size]
    for path in paths[1:]:
        if path not in depths:
            depths[path] = swap_tm(depths[path[:-1]], path[-1])
    pre_grad = call(
        grad_kernel,
        jax.ShapeDtypeStruct((width + 16, rows), BF16),
        [(VMEM, keep), (VMEM, arrived), (VMEM, lost), (VMEM, slope)],
        0.3,
    )
    groups = [[(), (0,)], [path for path in paths[1:] if path[-1] != 0]]
    groups.append([path for path in paths if path not in groups[0] + groups[1]])

    def operands(group):
        return [(VMEM, grads[path]) for path in group] + [(VMEM, depths[path]) for path in group]

    grads = {(): pre_grad}
    for path in groups[0][1:] + groups[1]:
        grads[path] = swap_tm(grads[path[:-1]], path[-1])
    total_shape = jax.ShapeDtypeStruct((width, feats), F32)
    total = call(
        functools.partial(early_kernel, len(groups[0]), width), total_shape, operands(groups[0]), 0.3
    )
    top = groups[1][-1]
    grad_readout = call(
        functools.partial(readout_kernel, blocks),
        jax.ShapeDtypeStruct((share, slots), F32),
        [(SMEM, block_subject), (VMEM, raw_keep), (VMEM, raw_came), (VMEM, own_gains)],
        4.0,
    )
    grads[top], total, grad_readout = lax.optimization_barrier(
        (grads[top], total, grad_readout)
    )
    for path in groups[2]:
        grads[path] = swap_tm(grads[path[:-1]], path[-1])
    total = call(
        functools.partial(later_kernel, len(groups[1]), width),
        total_shape,
        [(VMEM, total)] + operands(groups[1]),
        0.3,
    )
    others = groups[0] + groups[1]
    ins = [(VMEM, total)] + [(VMEM, grads[path]) for path in others] + operands(groups[2])
    grad_point, loss_total = pl.pallas_call(
        functools.partial(
            last_kernel, len(others), len(groups[2]), width, 1.0 / (subjects * rows * tm_count)
        ),
        out_shape=(
            jax.ShapeDtypeStruct((feats, width), F32),
            jax.ShapeDtypeStruct((1, 1), F32),
        ),
        in_specs=[spec for spec, _ in ins],
        out_specs=(VMEM, SMEM),
        compiler_params=pltpu.CompilerParams(vmem_limit_bytes=16 << 20),
        cost_estimate=pl.CostEstimate(
            flops=int(1.15e9), bytes_accessed=1000000, transcendentals=0
        ),
    )(*[value for _, value in ins])
    return (loss_total.reshape(()), grad_readout, grad_point)


def solution(mesh):
    placed = (
        P("tm", None),
        P(),
        P(),
        P(),
        P(),
        P(None, "vox"),
        P(None, "vox"),
        P("vox"),
        P("vox"),
        P("tm", "vox"),
    )
    return jax.shard_map(
        functools.partial(shards, mesh.shape["tm"], mesh.shape["vox"]),
        mesh=mesh,
        in_specs=placed,
        out_specs=(P(), P("tm", "vox"), P(None, "vox")),
        check_vma=False,
    )
```

```python
import functools
import jax
import jax.numpy as jnp
from jax import lax
from jax.experimental import pallas as pl
from jax.experimental.pallas import tpu as pltpu
from jax.sharding import PartitionSpec as P

BLOCK_VOX = 128
KERNEL_TAPS = 3
TAP_SPACING = 8
HRF = 16
MARGIN = (KERNEL_TAPS - 1) * TAP_SPACING
F32 = jnp.float32
BF16 = jnp.bfloat16
NT = (((1,), (1,)), ((), ()))
VMEM = pl.BlockSpec(memory_space=pltpu.VMEM)
SMEM = pl.BlockSpec(memory_space=pltpu.SMEM)
HBM = pl.BlockSpec(memory_space=pltpu.HBM)


def call(body, outs, ins, micros, scratch=()):
    return pl.pallas_call(
        body,
        out_shape=outs,
        in_specs=[spec for spec, _ in ins],
        out_specs=jax.tree.map(lambda _: VMEM, outs),
        scratch_shapes=scratch,
        compiler_params=pltpu.CompilerParams(vmem_limit_bytes=16 << 20),
        cost_estimate=pl.CostEstimate(
            flops=int(micros * 1.15e9), bytes_accessed=int(micros * 1e6), transcendentals=0
        ),
    )(*[value for _, value in ins])


def session_starts(ends, time):
    start = jnp.zeros_like(time)
    for end in ends:
        start = jnp.where(time >= end, end, start)
    return start


def session_stops(ends, time):
    stop = jnp.zeros_like(time)
    for end in reversed(ends):
        stop = jnp.where(time < end, end, stop)
    return stop


def facts_of(ref, blocks):
    row = [ref[at : at + 1, :] for at in range(ref.shape[0])]
    return row[:blocks], row[blocks : 2 * blocks], row[2 * blocks :]


def pack_kernel(
    rows,
    blocks,
    subject_hbm,
    live_hbm,
    lengths_hbm,
    clip_ref,
    bold_ref,
    payload_ref,
    ends_ref,
    facts_ref,
    subject_ref,
    live_ref,
    lengths_ref,
    sems,
):
    slots = bold_ref.shape[1]
    tail = 2 * MARGIN
    moves = [
        (clip_ref.at[pl.ds(rows - tail, tail), :], payload_ref.at[pl.ds(0, tail), :]),
        (clip_ref.at[pl.ds(0, MARGIN), :], payload_ref.at[pl.ds(tail, MARGIN), :]),
        (
            bold_ref.at[pl.ds(0, MARGIN), :],
            payload_ref.at[pl.ds(tail + MARGIN, MARGIN), pl.ds(0, slots)],
        ),
        (subject_hbm, subject_ref),
        (live_hbm, live_ref),
        (lengths_hbm, lengths_ref),
    ]
    copies = [pltpu.make_async_copy(*move, sems.at[at]) for at, move in enumerate(moves)]
    for copy in copies:
        copy.start()
    payload_ref[3 * MARGIN :, slots:] = jnp.zeros_like(payload_ref[3 * MARGIN :, slots:])
    for copy in copies[3:]:
        copy.wait()
    row = lax.broadcasted_iota(jnp.int32, ends_ref.shape, 0)
    last = blocks - 1
    ends = jnp.where(row == 0, subject_ref[0], live_ref[0])
    ends = jnp.where(row == 2, subject_ref[last], ends)
    ends_ref[...] = jnp.where(row == 3, live_ref[last], ends)
    values = [subject_ref[b] for b in range(blocks)] + [live_ref[b] for b in range(blocks)]
    end = jnp.int32(0)
    for at in range(lengths_ref.shape[0]):
        end = end + lengths_ref[at]
        values.append(end)
    row = lax.broadcasted_iota(jnp.int32, facts_ref.shape, 0)
    facts = jnp.full(facts_ref.shape, end, jnp.int32)
    for at, value in enumerate(values):
        facts = jnp.where(row == at, value, facts)
    facts_ref[...] = facts
    for copy in copies[:3]:
        copy.wait()


def conv_kernel(
    rows, blocks, facts_ref, clip_ref, near_ref, far_ref, taps_ref, depth_ref, deep_ref, ext
):
    feats = clip_ref.shape[1]
    odd = lax.axis_index("tm") % 2
    ext[2 * MARGIN : 2 * MARGIN + rows, :] = clip_ref[...]

    @pl.when(odd == 0)
    def _():
        ext[: 2 * MARGIN, :] = far_ref[: 2 * MARGIN, :]
        ext[2 * MARGIN + rows :, :] = near_ref[2 * MARGIN : 3 * MARGIN, :]

    @pl.when(odd == 1)
    def _():
        ext[: 2 * MARGIN, :] = near_ref[: 2 * MARGIN, :]
        ext[2 * MARGIN + rows :, :] = far_ref[2 * MARGIN : 3 * MARGIN, :]

    first = lax.axis_index("tm") * rows - MARGIN
    session_ends = facts_of(facts_ref, blocks)[2]
    taps = [taps_ref[k : k + 1, :] for k in range(KERNEL_TAPS)]
    for at in range(0, rows + 2 * MARGIN, 16):
        time = first + at + lax.broadcasted_iota(jnp.int32, (16, 128), 0)
        since = time - session_starts(session_ends, time)
        values = ext[at : at + 32, :].astype(F32)
        total = taps[0] * values[16:32]
        for k in range(1, KERNEL_TAPS):
            valid = (since >= k * TAP_SPACING).astype(F32)
            shift = MARGIN - k * TAP_SPACING
            moved = values[shift : shift + 16] * jnp.tile(valid, (1, feats // 128))
            total = total + taps[k] * moved
        deep_ref[at : at + 16, :] = total.astype(BF16)
    depth_ref[...] = deep_ref[MARGIN : MARGIN + rows, :]


def core_kernel(
    rows,
    blocks,
    clip_ref,
    near_ref,
    far_ref,
    deep_ref,
    point_ref,
    facts_ref,
    gains_ref,
    weight_ref,
    core_ref,
    effective_ref,
    response_ref,
    ext,
):
    feats = clip_ref.shape[1]
    odd = lax.axis_index("tm") % 2
    ext[MARGIN : MARGIN + rows, :] = clip_ref[...]

    @pl.when(odd == 0)
    def _():
        ext[:MARGIN, :] = far_ref[MARGIN : 2 * MARGIN, :]
        ext[MARGIN + rows :, :] = near_ref[2 * MARGIN : 3 * MARGIN, :]

    @pl.when(odd == 1)
    def _():
        ext[:MARGIN, :] = near_ref[MARGIN : 2 * MARGIN, :]
        ext[MARGIN + rows :, :] = far_ref[2 * MARGIN : 3 * MARGIN, :]

    slots = blocks * BLOCK_VOX
    subjects = gains_ref.shape[0]
    whole = gains_ref[...]
    high = whole.astype(BF16).astype(F32)
    middle = (whole - high).astype(BF16).astype(F32)
    low = whole - high - middle
    terms = jnp.concatenate([high, middle, low], axis=0).astype(BF16)
    owner = jnp.concatenate(facts_of(facts_ref, blocks)[0], axis=1)
    row = lax.broadcasted_iota(jnp.int32, (3 * subjects, slots), 0) % subjects
    pick = jnp.where(row == owner, 1.0, 0.0).astype(BF16)
    scale = lax.dot_general(
        terms, pick, (((0,), (0,)), ((), ())), preferred_element_type=F32
    )
    effective_ref[...] = (weight_ref[...].astype(F32) * scale).astype(BF16)
    for col in range(0, feats, 256):
        lanes = slice(col, col + 256)
        act = jnp.dot(deep_ref[...], point_ref[:, lanes], preferred_element_type=F32)
        core_ref[:, lanes] = (ext[:, lanes].astype(F32) + jax.nn.gelu(act)).astype(BF16)
    for b in range(0, blocks, 2):
        many = min(2, blocks - b)
        lanes = slice(b * BLOCK_VOX, (b + many) * BLOCK_VOX)
        part = jnp.dot(core_ref[...], effective_ref[:, lanes], preferred_element_type=F32)
        part = part.astype(BF16).astype(F32)
        for c in range(many):
            response_ref[b + c] = part[:, c * BLOCK_VOX : (c + 1) * BLOCK_VOX]


def block_at(position, bits):
    return sum(
        ((position >> (len(bits) - 1 - s)) & 1) << bits[s] for s in range(len(bits))
    )


def picked(position, orders):
    even, odd = (block_at(position, bits) for bits in orders)
    mask = jnp.where(lax.axis_index("tm") % 2 == 0, even, odd)
    return lax.axis_index("vox") ^ mask


def spread_taps(hrf_ref, taps):
    for k in range(HRF):
        taps[k] = jnp.broadcast_to(hrf_ref[k : k + 1, :], taps.shape[1:])


def filtered(at, blocks, taps, limit, source, base, step):
    pairs = [(b, h) for b in range(blocks) for h in (0, 8)]
    depth = {h: limit[at + h : at + h + 8, :] for h in (0, 8)}
    total = {}
    for b, h in pairs:
        lanes = slice(b * BLOCK_VOX, (b + 1) * BLOCK_VOX)
        row = at + h + base
        total[b, h] = taps[0, :, lanes] * source[b, row : row + 8, :]
    for k in range(1, HRF):
        valid = {h: depth[h] >= k for h in (0, 8)}
        for b, h in pairs:
            lanes = slice(b * BLOCK_VOX, (b + 1) * BLOCK_VOX)
            row = at + h + base + step * k
            moved = jnp.where(valid[h], source[b, row : row + 8, :], 0.0)
            total[b, h] = total[b, h] + taps[k, :, lanes] * moved
    return total


def forward_kernel(
    rows, blocks, facts_ref, response_ref, hrf_ref, bold_ref, near_ref, far_ref, misfit_ref, bold, since, taps
):
    lead_rows = rows + MARGIN
    slots = blocks * BLOCK_VOX
    odd = lax.axis_index("tm") % 2
    bold[:rows, :] = bold_ref[...]

    @pl.when(odd == 0)
    def _():
        bold[rows:, :] = near_ref[3 * MARGIN :, :slots]

    @pl.when(odd == 1)
    def _():
        bold[rows:, :] = far_ref[3 * MARGIN :, :slots]

    first = lax.axis_index("tm") * rows
    time = first + lax.broadcasted_iota(jnp.int32, (lead_rows, BLOCK_VOX), 0)
    since[...] = time - session_starts(facts_of(facts_ref, blocks)[2], time)
    spread_taps(hrf_ref, taps)
    for at in range(0, lead_rows, 16):
        total = filtered(at, blocks, taps, since, response_ref, MARGIN, -1)
        for b in range(blocks):
            target = bold[at : at + 16, b * BLOCK_VOX : (b + 1) * BLOCK_VOX].astype(F32)
            for h in (0, 8):
                misfit_ref[b, at + h : at + h + 8, :] = total[b, h] - target[h : h + 8]


def backward_kernel(
    rows,
    blocks,
    orders,
    width,
    facts_ref,
    mine_ref,
    twin_ref,
    misfit_ref,
    effective_ref,
    hrf_ref,
    half_ref,
    send_ref,
    loss_ref,
    grads,
    left,
    taps,
):
    lead_rows = rows + MARGIN
    own_subjects, own_lives, session_ends = facts_of(facts_ref, blocks)
    first_core = lax.axis_index("tm") % 2 == 0
    low = jnp.where(first_core, mine_ref[...], twin_ref[...])
    high = jnp.where(first_core, twin_ref[...], mine_ref[...])
    even_vox = lax.axis_index("vox") % 2 == 0
    before = jnp.where(even_vox, high, low)
    after = jnp.where(even_vox, low, high)
    subjects = [before[2:3]] + own_subjects + [after[0:1]]
    lives = [before[3:4]] + own_lives + [after[1:2]]
    lane = lax.broadcasted_iota(jnp.int32, (8, BLOCK_VOX), 1)
    lost = jnp.zeros((8, BLOCK_VOX), F32)
    for b in range(blocks):
        count = lives[b + 1]
        count = count + jnp.where(subjects[b] == subjects[b + 1], lives[b], 0)
        count = count + jnp.where(subjects[b + 2] == subjects[b + 1], lives[b + 2], 0)
        inverse = 1.0 / jnp.maximum(count, 1).astype(F32)
        weight = jnp.where(lane < lives[b + 1], inverse, 0.0)
        double = 2.0 * weight
        for at in range(0, lead_rows, 8):
            misfit = misfit_ref[b, at : at + 8, :]
            grads[b, at : at + 8, :] = double * misfit
            if at < rows:
                lost = lost + weight * misfit * misfit
    loss_ref[...] = lost
    time = lax.axis_index("tm") * rows + lax.broadcasted_iota(jnp.int32, (rows, BLOCK_VOX), 0)
    left[...] = session_stops(session_ends, time) - 1 - time
    spread_taps(hrf_ref, taps)
    for at in range(0, rows, 16):
        total = filtered(at, blocks, taps, left, grads, 0, 1)
        for b in range(blocks):
            half_ref[at : at + 16, b * BLOCK_VOX : (b + 1) * BLOCK_VOX] = jnp.concatenate(
                [total[b, 0], total[b, 8]], axis=0
            ).astype(BF16)
    halves = 1 << (len(orders[0]) - 1)
    send_ref[halves * width :, :] = loss_pair(lost, rows)
    for p in range(halves):
        at = pl.multiple_of(picked(halves + p, orders) * width, width)
        send_ref[p * width : (p + 1) * width, :] = lax.dot_general(
            effective_ref[pl.ds(at, width), :], half_ref[...], NT, preferred_element_type=F32
        ).astype(BF16)


def rest_kernel(
    rows, orders, width, tm_bits, share, core_ref, effective_ref, half_ref, keep_ref, out_ref, own_ref, flipped
):
    halves = 1 << (len(orders[0]) - 1)
    flipped[...] = jnp.transpose(core_ref[MARGIN : MARGIN + rows, :])
    pieces = 1 << len(tm_bits)
    for q in reversed(range(pieces)):
        at = pl.multiple_of((lax.axis_index("tm") ^ block_at(q, tm_bits)) * share, share)
        part = jnp.dot(flipped[pl.ds(at, share), :], half_ref[...], preferred_element_type=F32)
        if q >= pieces // 2:
            slot = q - pieces // 2
            out_ref[slot * share : (slot + 1) * share, :] = part.astype(BF16)
        else:
            own_ref[q * share : (q + 1) * share, :] = part
    for p in range(halves):
        at = pl.multiple_of(picked(p, orders) * width, width)
        keep_ref[p * width : (p + 1) * width, :] = lax.dot_general(
            effective_ref[pl.ds(at, width), :], half_ref[...], NT, preferred_element_type=F32
        )


def slope_kernel(point_ref, depth_ref, slope_ref):
    act = lax.dot_general(
        point_ref[...], depth_ref[...], (((0,), (1,)), ((), ())), preferred_element_type=F32
    )
    slope_ref[...] = jax.vjp(jax.nn.gelu, act)[1](jnp.ones_like(act))[0]


def loss_pair(value, width):
    high = value.astype(BF16).astype(F32)
    pair = jnp.concatenate([high, value - high], axis=0)
    pad = jnp.zeros((16, width - BLOCK_VOX), F32)
    return jnp.concatenate([pair, pad], axis=1).astype(BF16)


def grad_kernel(keep_ref, arrived_ref, lost_ref, slope_ref, out_ref):
    width = keep_ref.shape[0]
    total = keep_ref[...] + arrived_ref[:width, :].astype(F32)
    out_ref[:width, :] = (total * slope_ref[...]).astype(BF16)
    pair = arrived_ref[width:, :BLOCK_VOX].astype(F32)
    out_ref[width:, :] = loss_pair(lost_ref[...] + pair[:8] + pair[8:], keep_ref.shape[1])


def early_kernel(parts, width, *refs):
    grad_refs, depth_refs, (total_ref,) = refs[:parts], refs[parts : 2 * parts], refs[2 * parts :]
    for col in range(0, total_ref.shape[1], 256):
        lanes = slice(col, col + 256)
        total = None
        for grad_ref, depth_ref in zip(grad_refs, depth_refs):
            part = jnp.dot(
                grad_ref[:width, :], depth_ref[:, lanes], preferred_element_type=F32
            )
            total = part if total is None else total + part
        total_ref[:, lanes] = total


def later_kernel(parts, width, before_ref, *refs):
    grad_refs, depth_refs, (total_ref,) = refs[:parts], refs[parts : 2 * parts], refs[2 * parts :]
    for col in range(0, total_ref.shape[1], 256):
        lanes = slice(col, col + 256)
        total = before_ref[:, lanes]
        for grad_ref, depth_ref in zip(grad_refs, depth_refs):
            total = total + jnp.dot(
                grad_ref[:width, :], depth_ref[:, lanes], preferred_element_type=F32
            )
        total_ref[:, lanes] = total


def last_kernel(others, parts, width, scale, total_ref, *refs):
    other_refs = refs[:others]
    grad_refs = refs[others : others + parts]
    depth_refs = refs[others + parts : others + 2 * parts]
    point_ref, loss_ref = refs[others + 2 * parts :]
    lost = None
    for ref in other_refs + grad_refs:
        part = ref[width:, :BLOCK_VOX].astype(F32)
        lost = part if lost is None else lost + part
    loss_ref[0, 0] = jnp.sum(lost) * scale
    for col in range(0, total_ref.shape[1], 256):
        lanes = slice(col, col + 256)
        total = total_ref[:, lanes]
        for grad_ref, depth_ref in zip(grad_refs, depth_refs):
            total = total + jnp.dot(
                grad_ref[:width, :], depth_ref[:, lanes], preferred_element_type=F32
            )
        point_ref[lanes, :] = jnp.transpose(total)


def readout_kernel(blocks, subject_ref, keep_ref, arrived_ref, gains_ref, out_ref):
    rows = [gains_ref[pl.ds(subject_ref[b], 1), :] for b in range(blocks)]
    rows += [rows[-1]] * (-blocks % 8)
    cols = jnp.transpose(jnp.concatenate(rows, axis=0))
    for b in range(blocks):
        lanes = slice(b * BLOCK_VOX, (b + 1) * BLOCK_VOX)
        total = keep_ref[:, lanes] + arrived_ref[:, lanes].astype(F32)
        out_ref[:, lanes] = total * cols[:, b : b + 1]


def shards(
    tm_count,
    vox_count,
    clip_features,
    depth_kernel,
    point_weight,
    session_lengths,
    subject_feature_gains,
    readout_weight,
    hrf_kernel,
    block_subject,
    block_live,
    bold_target,
):
    rows, feats = clip_features.shape
    slots = readout_weight.shape[1]
    blocks = slots // BLOCK_VOX
    subjects = subject_feature_gains.shape[0]
    width = feats // vox_count
    share = feats // tm_count
    vox_bits = list(range(vox_count.bit_length() - 1))
    orders = (vox_bits, [vox_bits[1], vox_bits[0]] + vox_bits[2:])
    tm_bits = list(range(tm_count.bit_length() - 1))

    def swap_tm(value, bit):
        return lax.ppermute(value, "tm", [(i, i ^ (1 << bit)) for i in range(tm_count)])

    def across(value, partner):
        pairs = []
        for t in range(tm_count):
            for v in range(vox_count):
                to = partner(t, v)
                if to is not None:
                    pairs.append((t * vox_count + v, to[0] * vox_count + to[1]))
        return lax.ppermute(value, ("tm", "vox"), pairs)

    def next_tm(t, v):
        other = t + 1 if t % 2 else t - 1
        return (other, v) if 0 <= other < tm_count else None

    def next_vox(t, v):
        if t % 2 == 0:
            return (t, v ^ 1)
        other = v + 1 if v % 2 else v - 1
        return (t, other) if 0 <= other < vox_count else None

    fact_rows = 2 * blocks + session_lengths.shape[0]
    fact_rows += -fact_rows % 8
    payload, ends, facts = pl.pallas_call(
        functools.partial(pack_kernel, rows, blocks),
        out_shape=(
            pltpu.VMEM((4 * MARGIN, feats), BF16),
            pltpu.VMEM((8, BLOCK_VOX), jnp.int32),
            pltpu.VMEM((fact_rows, BLOCK_VOX), jnp.int32),
        ),
        in_specs=[HBM] * 5,
        out_specs=(VMEM, VMEM, VMEM),
        scratch_shapes=[
            pltpu.SMEM((blocks,), jnp.int32),
            pltpu.SMEM((blocks,), jnp.int32),
            pltpu.SMEM(session_lengths.shape, jnp.int32),
            pltpu.SemaphoreType.DMA((6,)),
        ],
        cost_estimate=pl.CostEstimate(
            flops=int(6 * 1.15e9), bytes_accessed=1000000, transcendentals=0
        ),
    )(
        *[
            pltpu.with_memory_space_constraint(value, pltpu.HBM)
            for value in (block_subject, block_live, session_lengths, clip_features, bold_target)
        ]
    )
    far = across(payload, next_tm)
    mine = across(ends, next_vox)
    near = swap_tm(payload, 0)

    halos = [(VMEM, clip_features), (VMEM, near), (VMEM, far)]
    depth_half, deep = call(
        functools.partial(conv_kernel, rows, blocks),
        (
            jax.ShapeDtypeStruct((rows, feats), BF16),
            jax.ShapeDtypeStruct((rows + 2 * MARGIN, feats), BF16),
        ),
        [(VMEM, facts)] + halos + [(VMEM, depth_kernel)],
        0.1,
        [pltpu.VMEM((rows + 3 * MARGIN, feats), BF16)],
    )
    core_out, effective, response = call(
        functools.partial(core_kernel, rows, blocks),
        (
            jax.ShapeDtypeStruct((rows + 2 * MARGIN, feats), BF16),
            jax.ShapeDtypeStruct((feats, slots), BF16),
            jax.ShapeDtypeStruct((blocks, rows + 2 * MARGIN, BLOCK_VOX), F32),
        ),
        halos
        + [(VMEM, deep), (VMEM, point_weight), (VMEM, facts)]
        + [(VMEM, subject_feature_gains), (VMEM, readout_weight)],
        1.0,
        [pltpu.VMEM((rows + 2 * MARGIN, feats), BF16)],
    )
    response, mine = lax.optimization_barrier((response, mine))
    twin = swap_tm(mine, 0)
    misfit = call(
        functools.partial(forward_kernel, rows, blocks),
        jax.ShapeDtypeStruct((blocks, rows + MARGIN, BLOCK_VOX), F32),
        [
            (VMEM, facts),
            (VMEM, response),
            (VMEM, hrf_kernel),
            (VMEM, bold_target),
            (VMEM, near),
            (VMEM, far),
        ],
        1.5,
        [
            pltpu.VMEM((rows + MARGIN, slots), BF16),
            pltpu.VMEM((rows + MARGIN, BLOCK_VOX), jnp.int32),
            pltpu.VMEM((HRF, 8, slots), F32),
        ],
    )
    half, send, lost = call(
        functools.partial(backward_kernel, rows, blocks, orders, width),
        (
            jax.ShapeDtypeStruct((rows, slots), BF16),
            jax.ShapeDtypeStruct((feats // 2 + 16, rows), BF16),
            jax.ShapeDtypeStruct((8, BLOCK_VOX), F32),
        ),
        [
            (VMEM, facts),
            (VMEM, mine),
            (VMEM, twin),
            (VMEM, misfit),
            (VMEM, effective),
            (VMEM, hrf_kernel),
        ],
        2.5,
        [
            pltpu.VMEM((blocks, rows + MARGIN, BLOCK_VOX), F32),
            pltpu.VMEM((rows, BLOCK_VOX), jnp.int32),
            pltpu.VMEM((HRF, 8, slots), F32),
        ],
    )
    keep, raw_send, raw_keep = call(
        functools.partial(rest_kernel, rows, orders, width, tm_bits, share),
        (
            jax.ShapeDtypeStruct((feats // 2, rows), F32),
            jax.ShapeDtypeStruct((feats // 2, slots), BF16),
            jax.ShapeDtypeStruct((feats // 2, slots), F32),
        ),
        [(VMEM, core_out), (VMEM, effective), (VMEM, half)],
        1.1,
        [pltpu.VMEM((feats, rows), BF16)],
    )

    def loss_rows(value):
        high = lax.reduce_precision(value, 8, 7)
        pair = jnp.concatenate([high, value - high], axis=0)
        return jnp.pad(pair, ((0, 0), (0, rows - BLOCK_VOX))).astype(BF16)

    def loss_of(arrived):
        pair = arrived[:, :BLOCK_VOX].astype(F32)
        return pair[:8] + pair[8:]

    col = lax.axis_index("vox") * width
    point_cols = lax.dynamic_slice_in_dim(point_weight, col, width, 1)
    slope = call(
        slope_kernel,
        jax.ShapeDtypeStruct((width, rows), F32),
        [(VMEM, point_cols), (VMEM, depth_half)],
        0.7,
    )
    own_gains = lax.dynamic_slice_in_dim(
        subject_feature_gains, lax.axis_index("tm") * share, share, 1
    )
    stages = len(vox_bits)
    paths = [()]
    for bit in reversed(tm_bits):
        paths = paths + [path + (bit,) for path in paths]
    depths = {(): depth_half}
    first = [(bit,) for bit in reversed(tm_bits)]
    for path in first:
        depths[path] = swap_tm(depth_half, path[0])
    raw_came = swap_tm(raw_send, tm_bits[0])
    for stage in range(stages):
        arrived = across(send, lambda t, v: (t, v ^ (1 << orders[t % 2][stage])))
        if stage == 0:
            held = lax.optimization_barrier((arrived, *[depths[path] for path in first]))
            arrived = held[0]
            depths.update(zip(first, held[1:]))
        if stage == min(1, stages - 1):
            for bit in tm_bits[1:]:
                raw_keep = raw_keep + raw_came.astype(F32)
                size = raw_keep.shape[0] // 2
                raw_send, raw_keep = raw_keep[size:].astype(BF16), raw_keep[:size]
                raw_came = swap_tm(raw_send, bit)
            arrived, raw_keep, slope, own_gains = lax.optimization_barrier(
                (arrived, raw_keep, slope, own_gains)
            )
        if stage + 1 < stages:
            size = keep.shape[0] // 2
            keep = keep + arrived[: 2 * size].astype(F32)
            lost = lost + loss_of(arrived[2 * size :])
            send = jnp.concatenate([keep[size:].astype(BF16), loss_rows(lost)], axis=0)
            keep = keep[:size]
    for path in paths[1:]:
        if path not in depths:
            depths[path] = swap_tm(depths[path[:-1]], path[-1])
    held = lax.optimization_barrier((arrived, *[depths[path] for path in paths[1:]]))
    arrived = held[0]
    depths.update(zip(paths[1:], held[1:]))
    pre_grad = call(
        grad_kernel,
        jax.ShapeDtypeStruct((width + 16, rows), BF16),
        [(VMEM, keep), (VMEM, arrived), (VMEM, lost), (VMEM, slope)],
        0.3,
    )
    groups = [[(), (0,)], [path for path in paths[1:] if path[-1] != 0]]
    groups.append([path for path in paths if path not in groups[0] + groups[1]])

    def operands(group):
        return [(VMEM, grads[path]) for path in group] + [(VMEM, depths[path]) for path in group]

    grads = {(): pre_grad}
    for path in groups[0][1:] + groups[1]:
        grads[path] = swap_tm(grads[path[:-1]], path[-1])
    total_shape = jax.ShapeDtypeStruct((width, feats), F32)
    total = call(
        functools.partial(early_kernel, len(groups[0]), width), total_shape, operands(groups[0]), 0.3
    )
    top = groups[1][-1]
    grad_readout = call(
        functools.partial(readout_kernel, blocks),
        jax.ShapeDtypeStruct((share, slots), F32),
        [(SMEM, block_subject), (VMEM, raw_keep), (VMEM, raw_came), (VMEM, own_gains)],
        4.0,
    )
    grads[top], total, grad_readout = lax.optimization_barrier(
        (grads[top], total, grad_readout)
    )
    for path in groups[2]:
        grads[path] = swap_tm(grads[path[:-1]], path[-1])
    total = call(
        functools.partial(later_kernel, len(groups[1]), width),
        total_shape,
        [(VMEM, total)] + operands(groups[1]),
        0.3,
    )
    others = groups[0] + groups[1]
    ins = [(VMEM, total)] + [(VMEM, grads[path]) for path in others] + operands(groups[2])
    grad_point, loss_total = pl.pallas_call(
        functools.partial(
            last_kernel, len(others), len(groups[2]), width, 1.0 / (subjects * rows * tm_count)
        ),
        out_shape=(
            jax.ShapeDtypeStruct((feats, width), F32),
            jax.ShapeDtypeStruct((1, 1), F32),
        ),
        in_specs=[spec for spec, _ in ins],
        out_specs=(VMEM, SMEM),
        compiler_params=pltpu.CompilerParams(vmem_limit_bytes=16 << 20),
        cost_estimate=pl.CostEstimate(
            flops=int(1.15e9), bytes_accessed=1000000, transcendentals=0
        ),
    )(*[value for _, value in ins])
    return (loss_total.reshape(()), grad_readout, grad_point)


def solution(mesh):
    placed = (
        P("tm", None),
        P(),
        P(),
        P(),
        P(),
        P(None, "vox"),
        P(None, "vox"),
        P("vox"),
        P("vox"),
        P("tm", "vox"),
    )
    return jax.shard_map(
        functools.partial(shards, mesh.shape["tm"], mesh.shape["vox"]),
        mesh=mesh,
        in_specs=placed,
        out_specs=(P(), P("tm", "vox"), P(None, "vox")),
        check_vma=False,
    )
```
